32 devices in a mesh: chaos: 4 (over z), gx: 4 (over y, x), gy: 2 (over core).
Axes of the slice: x: 2, y: 2, z: 4, core: 2. Of those that a mesh axis runs over, the one named last changes fastest.
Arguments:
- lam_start: float32 [286, 16, 512], P(None, ('chaos', 'gy'), 'gx'), may hold values from -6 to 6
- adj_source: float32 [286, 16, 512], P(None, ('chaos', 'gy'), 'gx'), may hold values from -6 to 6
- coef_points: float32 [512, 4, 4, 512], P('chaos', None, 'gy', 'gx'), may hold values from 0.1 to 1
- quad_index: int32 [512, 10], replicated, may hold values from 0 to 3
- mode_index: int32 [286, 10], replicated, may hold values from 0 to 3, as said below
Outputs:
- lam_end: float32 [286, 16, 512], P(None, ('chaos', 'gy'), 'gx')
The draws below stay inside these ranges and needn't reach their ends.
Inputs may be any that keep to these rules, and one draw needn't show every extreme that they name: `mode_index`: each row is a multi-index whose degrees sum to at most 3; each such multi-index of 10 inputs appears exactly once.
All inputs are finite; a program needn't handle non-finite values.
Results may differ from the reference program's by a relative error of at most 0.00011.
Values sent between devices are 32-bit elements; how exact they have to be, the bound alone decides.
A program may use at most 64 MiB of HBM per device.

```python
import math
import jax
import jax.numpy as jnp
import numpy as np
from jax import lax

NINP = 10
P_SIZE = 286
Q = 512
STEPS = 2
NX = 512
NYB = 4
NY = 16
N_CHAOS = 4


def index_list(inputs):
    entries = [[0] * inputs]
    for axis_one in range(inputs):
        degree_row = [0] * inputs
        degree_row[axis_one] += 1
        entries.append(degree_row)
    for axis_one in range(inputs):
        for axis_two in range(axis_one, inputs):
            degree_row = [0] * inputs
            degree_row[axis_one] += 1
            degree_row[axis_two] += 1
            entries.append(degree_row)
    for axis_one in range(inputs):
        for axis_two in range(axis_one, inputs):
            for axis_three in range(axis_two, inputs):
                degree_row = [0] * inputs
                degree_row[axis_one] += 1
                degree_row[axis_two] += 1
                degree_row[axis_three] += 1
                entries.append(degree_row)
    return np.array(entries, dtype=np.int32)


def draw_mode_index(key, part):
    table = jnp.asarray(index_list(NINP), jnp.int32)
    order = jax.random.permutation(key, table.shape[0])
    return table[order]


def place_ends(values, rng, low, largest):
    longest = values.shape.index(max(values.shape))
    spots = []
    for shift in (0, 1):
        where = [jax.random.randint(jax.random.fold_in(rng, axis), (), 0, length) for axis, length in enumerate(values.shape)]
        where[longest] = (where[longest] + shift) % values.shape[longest]
        spots.append(tuple(where))
    return values.at[spots[0]].set(low).at[spots[1]].set(largest)


def block_scale(rng, shape, pieces, low, top_value):
    level, own = 1.0, jax.random.fold_in(rng, 6)
    for axis_at, shards_of in pieces:
        steps = jnp.exp(jax.random.uniform(jax.random.fold_in(own, axis_at), (shards_of,), jnp.float32, low / len(pieces), top_value / len(pieces)))
        level = level * jnp.repeat(steps, shape[axis_at] // shards_of).reshape([-1 if axis == axis_at else 1 for axis in range(len(shape))])
    return level


def bell_draw(own_key, dims, spread, limit, pieces=(), held_as=jnp.bfloat16):
    values = spread * jax.random.normal(own_key, dims, jnp.float32)
    if pieces:
        values = values * block_scale(own_key, dims, pieces, -0.22, 0.18)
    return jnp.clip(values, -limit, limit).astype(held_as)


def setup_inputs(seed: int = 0) -> dict:
    arg_keys = jax.random.split(jax.random.key(seed), 6)
    return {
        "lam_start": bell_draw(arg_keys[0], (P_SIZE, NY, NX), 1.0, 6.0, ((1, 8), (2, 4)), jnp.float32),
        "adj_source": bell_draw(arg_keys[1], (P_SIZE, NY, NX), 1.0, 6.0, ((1, 8), (2, 4)), jnp.float32),
        "coef_points": jnp.clip(jnp.exp(math.log(1.0) - 2.3025851 * jax.random.uniform(arg_keys[2], (Q, N_CHAOS, NYB, NX), jnp.float32) ** block_scale(arg_keys[2], (Q, N_CHAOS, NYB, NX), ((0, 4), (2, 2), (3, 4)), -0.2, 0.2)), 0.1, 1.0),
        "quad_index": place_ends(jax.random.randint(arg_keys[3], (Q, NINP), 0, 4), jax.random.fold_in(arg_keys[3], 1), 0, 3).astype(jnp.int32),
        "mode_index": draw_mode_index(jax.random.fold_in(arg_keys[5], 71), 0),
    }


gauss_nodes = (-2.3344142183389773, -0.7419637843027259, 0.7419637843027259, 2.3344142183389773)
gauss_weights = (0.04587585476806849, 0.4541241452319315, 0.4541241452319315, 0.04587585476806849)
mass_shift = 1.0
relax_rate = 0.2
top_prec = lax.Precision.HIGHEST

def tables(quad_index, mode_index):
    node_vals = jnp.array(gauss_nodes, jnp.float32)
    node_wts = jnp.array(gauss_weights, jnp.float32)
    hermite = jnp.stack([jnp.ones_like(node_vals), node_vals, (node_vals * node_vals - 1.0) / math.sqrt(2.0), (node_vals * node_vals * node_vals - 3.0 * node_vals) / math.sqrt(6.0)], 0)
    levels = jnp.arange(4, dtype=jnp.int32)
    quad_hot = (quad_index[:, :, None] == levels[None, None, :]).astype(jnp.float32)
    mode_hot = (mode_index[:, :, None] == levels[None, None, :]).astype(jnp.float32)
    at_nodes = jnp.einsum('qdk,nk->qdn', quad_hot, hermite, precision=top_prec)
    factors = jnp.einsum('qdn,pdn->qpd', at_nodes, mode_hot, precision=top_prec)
    chaos_basis = jnp.prod(factors, axis=2)
    point_wts = jnp.prod(lax.optimization_barrier(jnp.sum(quad_hot * node_wts[None, None, :], axis=2)), axis=1)
    point_wts = point_wts / jnp.sum(point_wts)
    back_map = chaos_basis * point_wts[:, None]
    return (chaos_basis, back_map)

def operate(current, coef_rows, chaos_basis, back_map):
    padded_y = jnp.pad(current, ((0, 0), (1, 1), (0, 0)))

    def point_flux(row_start):
        slab = lax.dynamic_slice_in_dim(padded_y, row_start, NYB + 2, 1)
        center = slab[:, 1:-1]
        grad_x = (jnp.roll(center, -1, 2) - jnp.roll(center, 1, 2)) * 0.5
        grad_y = (slab[:, 2:] - slab[:, :-2]) * 0.5
        gradients = jnp.stack([grad_x, grad_y], 1)
        at_points = jnp.dot(chaos_basis, gradients.reshape(P_SIZE, -1), precision=top_prec, preferred_element_type=jnp.float32).reshape(Q, 2, NYB, NX)
        coef_block = lax.dynamic_slice_in_dim(coef_rows, row_start, NYB, 1)
        flux_points = at_points * coef_block[:, None]
        return jnp.dot(back_map.T, flux_points.reshape(Q, -1), precision=top_prec, preferred_element_type=jnp.float32).reshape(P_SIZE, 2, NYB, NX)
    starts = jnp.arange(N_CHAOS, dtype=jnp.int32) * NYB
    mapped = lax.map(point_flux, starts)
    fluxes = jnp.transpose(mapped, (1, 2, 0, 3, 4)).reshape(P_SIZE, 2, NY, NX)
    flux_x = fluxes[:, 0]
    flux_yp = jnp.pad(fluxes[:, 1], ((0, 0), (1, 1), (0, 0)))
    divergence = (jnp.roll(flux_x, -1, 2) - jnp.roll(flux_x, 1, 2)) * 0.5 + (flux_yp[:, 2:] - flux_yp[:, :-2]) * 0.5
    return mass_shift * current - divergence

def reference(lam_start, adj_source, coef_points, quad_index, mode_index):
    chaos_basis, back_map = tables(quad_index, mode_index)
    coef_rows = coef_points.reshape(Q, NY, NX)
    lam_now = lam_start
    for repeat in range(STEPS):
        lam_now = lam_now + relax_rate * (adj_source - operate(lam_now, coef_rows, chaos_basis, back_map))
    return lam_now
```

```python
import functools
import math

import jax
import jax.numpy as jnp
from jax import lax
from jax.experimental import pallas as pl
from jax.experimental.pallas import tpu as pltpu
from jax.sharding import PartitionSpec as P

STEPS = 2
FACTORS = 3

gauss_nodes = (-2.3344142183389773, -0.7419637843027259, 0.7419637843027259, 2.3344142183389773)
gauss_weights = (0.04587585476806849, 0.4541241452319315, 0.4541241452319315, 0.04587585476806849)
mass_shift = 1.0
relax_rate = 0.2
f32 = jnp.float32
bf16 = jnp.bfloat16


def split(x):
    high = x.astype(bf16)
    return high, (x - high.astype(f32)).astype(bf16)


def dot3(ah, al, bh, bl):
    dot = functools.partial(jnp.dot, preferred_element_type=f32)
    return dot(ah, bh) + (dot(ah, bl) + dot(al, bh))


def kernel(
    dims, lam_hbm, adj_hbm, coef_hbm, quad_hbm, mode_hbm, out_ref,
    lam_raw, adj_ref, quad_ref, mode_ref, kraw, ktmp, kfar, kmid, khalo, kedge, ksend, krecv,
    lam0, lam1, vhalo, vsend, vrecv, u, psi_h, psi_l, bt_h, bt_l, d_h, d_l, d_x,
    in_sem, main_send, main_recv, far_send, halo_send, halo_recv, edge_send, edge_recv, v_send, v_recv,
):
    n, ncore, ngx, inputs, modes, rows_p, wide, points, pts = dims
    z, x, c = lax.axis_index("chaos"), lax.axis_index("gx"), lax.axis_index("gy")
    count = n * ncore
    me = z * ncore + c
    above = lax.rem(me + 1, count)
    below = lax.rem(me + count - 1, count)
    has_above, has_below = me < count - 1, me > 0
    dev_above = {"chaos": lax.div(above, ncore), "gy": lax.rem(above, ncore)}
    dev_below = {"chaos": lax.div(below, ncore), "gy": lax.rem(below, ncore)}
    dev_right = {"gx": lax.rem(x + 1, ngx)}
    dev_left = {"gx": lax.rem(x + ngx - 1, ngx)}
    half = n // 2
    top, bottom = c == ncore - 1, c == 0
    mid_low = top & (z == half - 1)
    mid_high = bottom & (z == half)
    gives_up, gives_down = has_above & jnp.logical_not(mid_low), has_below & jnp.logical_not(mid_high)

    def remote(src, dst, ss, rs, dev):
        return pltpu.make_async_remote_copy(
            src_ref=src, dst_ref=dst, send_sem=ss, recv_sem=rs, device_id=dev,
            device_id_type=pl.DeviceIdType.MESH,
        )

    far_block = jnp.where(top, half - 1, half)
    get_own = pltpu.make_async_copy(coef_hbm.at[:, z], kraw.at[z], in_sem.at[0])
    get_far = pltpu.make_async_copy(coef_hbm.at[:, far_block], ktmp, in_sem.at[1])
    get_lam = pltpu.make_async_copy(lam_hbm, lam_raw, in_sem.at[2])
    get_quad = pltpu.make_async_copy(quad_hbm, quad_ref, in_sem.at[3])
    get_mode = pltpu.make_async_copy(mode_hbm, mode_ref, in_sem.at[4])
    get_adj = pltpu.make_async_copy(adj_hbm, adj_ref, in_sem.at[5])
    for get in (get_own, get_far, get_lam, get_quad, get_mode, get_adj):
        get.start()

    barrier = pltpu.get_barrier_semaphore()

    def greet(dev):
        pl.semaphore_signal(barrier, inc=1, device_id=dev, device_id_type=pl.DeviceIdType.MESH)

    def greet_line(i, carry):
        other = lax.rem(me + i, count)
        greet({"chaos": lax.div(other, ncore), "gy": lax.rem(other, ncore)})
        return carry

    lax.fori_loop(1, count, greet_line, 0, unroll=count <= 8)
    greet(dev_left)
    greet(dev_right)
    pl.semaphore_wait(barrier, count + 1)

    def main_copy(to):
        return remote(coef_hbm.at[:, to], kraw.at[z], main_send.at[to], main_recv.at[z], {"chaos": to})

    sign = 1 - 2 * lax.rem(z, 2)
    inner = (4 * z >= n) & (4 * z < 3 * n)
    outer_order = sorted(range(1, n), key=lambda k: (abs(2 * k - n), -k))
    inner_order = sorted(range(1, n), key=lambda k: (-abs(2 * k - n), k)) if n != 4 else [1, 2, 3]

    def partner(i):
        return lax.rem(z + n + sign * jnp.where(inner, inner_order[i], outer_order[i]), n)

    for i in range(n - 1):
        main_copy(partner(i)).start()

    far_up = remote(kfar, khalo.at[z, 0], far_send, halo_recv.at[0, z], {"chaos": half, "gy": 0})
    far_down = remote(kfar, khalo.at[z, 1], far_send, halo_recv.at[1, z], {"chaos": half - 1, "gy": ncore - 1})
    get_far.wait()

    @pl.when(top)
    def _():
        kfar[...] = ktmp[:, 1, :]
        far_up.start()

    @pl.when(bottom)
    def _():
        kfar[...] = ktmp[:, 0, :]
        far_down.start()

    def v_copies(step, p, src):
        return (
            remote(src.at[p], vhalo.at[step, 0, p], v_send.at[step, 0, p], v_recv.at[step, 0, p], dev_above),
            remote(src.at[p], vhalo.at[step, 1, p], v_send.at[step, 1, p], v_recv.at[step, 1, p], dev_below),
            remote(vsend.at[step, 0, p], vrecv.at[step, 1, p], v_send.at[step, 2, p], v_recv.at[step, 2, p], dev_left),
            remote(vsend.at[step, 1, p], vrecv.at[step, 0, p], v_send.at[step, 3, p], v_recv.at[step, 3, p], dev_right),
        )

    def start_v(step, p, src):
        up, down, left, right = v_copies(step, p, src)

        @pl.when(has_above)
        def _():
            up.start()

        @pl.when(has_below)
        def _():
            down.start()

        flipped = jnp.concatenate([src[p], jnp.zeros((wide - rows_p, 128), f32)], 0).T
        vsend[step, 0, p] = flipped[:8]
        vsend[step, 1, p] = flipped[120:]
        left.start()
        right.start()

    def halo_copies(j):
        return (
            remote(kmid.at[j, 1], khalo.at[j, 0], halo_send.at[0, j], halo_recv.at[0, j], dev_above),
            remote(kmid.at[j, 0], khalo.at[j, 1], halo_send.at[1, j], halo_recv.at[1, j], dev_below),
            remote(ksend.at[j, 0], krecv.at[j, 1], edge_send.at[0, j], edge_recv.at[0, j], dev_left),
            remote(ksend.at[j, 1], krecv.at[j, 0], edge_send.at[1, j], edge_recv.at[1, j], dev_right),
        )

    def forward(j):
        up, down, left, right = halo_copies(j)
        for r in range(2):
            kmid[j, r] = kraw[j, :, r, :]

        @pl.when(gives_up)
        def _():
            up.start()

        @pl.when(gives_down)
        def _():
            down.start()

        for r in range(2):
            flipped = kmid[j, r].T
            ksend[j, 0, r] = flipped[:8]
            ksend[j, 1, r] = flipped[120:]
        left.start()
        right.start()

    get_lam.wait()
    for p in range(2):
        lam0[p, :modes] = lam_raw[:, p, :]
        lam0[p, modes:] = jnp.zeros((rows_p - modes, 128), f32)
    for p in range(2):
        start_v(0, p, lam0)
    get_own.wait()
    forward(z)

    @pl.when(jnp.logical_not(has_below))
    def _():
        khalo[:, 0] = jnp.zeros((n, pts, 128), f32)
        vhalo[:, 0] = jnp.zeros((STEPS, 2, rows_p, 128), f32)

    @pl.when(jnp.logical_not(has_above))
    def _():
        khalo[:, 1] = jnp.zeros((n, pts, 128), f32)
        vhalo[:, 1] = jnp.zeros((STEPS, 2, rows_p, 128), f32)

    def tables():
        get_quad.wait()
        get_mode.wait()
        quad = quad_ref[...]
        each = jnp.where((quad == 0) | (quad == 3), gauss_weights[0], gauss_weights[1]).astype(f32)
        wts = each[:1]
        for d in range(1, inputs):
            wts = wts * each[d : d + 1]
        wts = wts / jnp.sum(wts, axis=1, keepdims=True) * 0.25
        node = jnp.where(
            quad == 0, gauss_nodes[0],
            jnp.where(quad == 1, gauss_nodes[1], jnp.where(quad == 2, gauss_nodes[2], gauss_nodes[3])),
        ).astype(f32)
        h2 = (node * node - 1.0) * (1.0 / math.sqrt(2.0))
        h3 = (node * node * node - 3.0 * node) * (1.0 / math.sqrt(6.0))
        fill = jnp.zeros((16 - inputs, points), f32)
        one = jnp.ones((16, points), f32)
        table = jnp.concatenate([node, fill, h2, fill, h3, fill, one], 0)
        first = table.astype(bf16).astype(f32)
        rest = table - first
        second = rest.astype(bf16).astype(f32)
        third = rest - second
        pieces = jnp.concatenate([first, second, third, jnp.zeros((64, points), f32)], 0)
        by_point = pieces.T.astype(bf16)

        deg = jnp.concatenate([mode_ref[...], jnp.zeros((inputs, wide - modes), jnp.int32)], 1)
        run = jnp.zeros((1, wide), jnp.int32)
        runs = []
        for d in range(inputs):
            run = run + jnp.where(deg[d : d + 1] > 0, 1, 0)
            runs.append(run)
        nth = jnp.concatenate(runs, 0)
        blank = jnp.zeros((16 - inputs, wide), f32)
        real = lax.broadcasted_iota(jnp.int32, (1, wide), 1) < modes
        product = None
        for i in range(FACTORS):
            picks = []
            for k in range(1, 4):
                picks.append(jnp.where((deg == k) & (nth == i + 1), 1.0, 0.0).astype(f32))
                picks.append(blank)
            picks.append(jnp.where((run <= i) & real, 1.0, 0.0).astype(f32))
            picks.append(jnp.zeros((15, wide), f32))
            pick = jnp.concatenate(picks, 0)
            pick = jnp.concatenate([pick, pick, pick, jnp.zeros((64, wide), f32)], 0).astype(bf16)
            factor = jnp.dot(by_point, pick, preferred_element_type=f32)
            product = factor if product is None else product * factor
        high, low = split(product)
        psi_h[...] = high
        psi_l[...] = low
        for i in range(points // 128):
            part = slice(i * 128, i * 128 + 128)
            flipped = product[part].T[:rows_p] * wts[:, part]
            high, low = split(flipped)
            bt_h[:, part] = high
            bt_l[:, part] = low

    tables()

    def to_points(p, at, first, second):
        vh, vl = split(jnp.concatenate([first, second], 1))
        res = dot3(psi_h[:, :rows_p], psi_l[:, :rows_p], vh, vl)
        u[p, at[0]] = res[:, :128]
        u[p, at[1]] = res[:, 128:]

    def own(step, p, src):
        left, right = v_copies(step, p, src)[2:]
        left.wait_recv()
        right.wait_recv()
        edge = jnp.concatenate([vrecv[step, 1, p], jnp.zeros((112, wide), f32), vrecv[step, 0, p]], 0).T[:rows_p]
        to_points(p, (1, 3), src[p], edge)

    def beside(step, p, src):
        up, down = v_copies(step, p, src)[:2]

        @pl.when(has_below)
        def _():
            up.wait_recv()

        @pl.when(has_above)
        def _():
            down.wait_recv()

        to_points(p, (0, 2), vhalo[step, 0, p], vhalo[step, 1, p])

    lane = lax.broadcasted_iota(jnp.int32, (1, 128), 1)
    is_first, is_last = lane == 0, lane == 127

    def across(p, j):
        rows = pl.ds(pl.multiple_of(j * pts, pts), pts)
        mid, end = u[p, 1, rows, :], u[p, 3, rows, :]
        a, b = pltpu.roll(mid, 127, 1), pltpu.roll(end, 127, 1)
        e, f = pltpu.roll(mid, 1, 1), pltpu.roll(end, 1, 1)
        fx = kmid[j, p] * (jnp.where(is_last, b, a) - jnp.where(is_first, f, e))
        fe = kedge[j, p] * (jnp.where(is_last, a, b) - jnp.where(is_first, e, f))
        nxt = jnp.where(is_last, pltpu.roll(fe, 127, 1), pltpu.roll(fx, 127, 1))
        prv = jnp.where(is_first, pltpu.roll(fe, 1, 1), pltpu.roll(fx, 1, 1))
        d_x[p, rows, :] = nxt - prv

    def along(p, j):
        rows = pl.ds(pl.multiple_of(j * pts, pts), pts)
        mid = u[p, 1, rows, :]
        k_low = khalo[j, 0] if p == 0 else kmid[j, 0]
        k_high = kmid[j, 1] if p == 0 else khalo[j, 1]
        flux = k_high * (u[p, 2, rows, :] - mid) - k_low * (mid - u[p, 0, rows, :])
        high, low = split(d_x[p, rows, :] + flux)
        d_h[p, rows, :] = high
        d_l[p, rows, :] = low

    def each_part(body):
        def step(j, carry):
            body(j)
            return carry

        lax.fori_loop(0, n, step, 0, unroll=n <= 4)

    def update(p, src, store):
        div = dot3(bt_h[...], bt_l[...], d_h[p], d_l[p])
        v = src[p, :modes]
        store(p, v + relax_rate * (adj_ref[:, p, :] - (mass_shift * v - div[:modes])))

    def receive(j):
        remote(coef_hbm.at[:, j], kraw.at[j], main_send.at[j], main_recv.at[j], {"chaos": j}).wait_recv()
        forward(j)

    def source(i):
        k = outer_order[-1 - i]
        return lax.rem(z + n + sign * (k if k % 2 else -k), n)

    own(0, 0, lam0)
    own(0, 1, lam0)
    for i in range(n - 1):
        receive(source(i))

    def arrive(j):
        left, right = halo_copies(j)[2:]
        left.wait_recv()
        right.wait_recv()
        for p in range(2):
            kedge[j, p] = jnp.concatenate([krecv[j, 1, p], jnp.zeros((112, pts), f32), krecv[j, 0, p]], 0).T
            across(p, j)

    each_part(arrive)

    def halo_arrive(p):
        def body(j):
            up, down = halo_copies(j)[:2]
            if p == 0:
                @pl.when(has_below)
                def _():
                    up.wait_recv()
            else:
                @pl.when(has_above)
                def _():
                    down.wait_recv()

        each_part(body)

    def keep_lam(p, value):
        lam1[p, :modes] = value
        lam1[p, modes:] = jnp.zeros((rows_p - modes, 128), f32)

    def give(p, value):
        out_ref[:, p, :] = value

    get_adj.wait()
    for p in range(2):
        beside(0, p, lam0)
        halo_arrive(p)
        each_part(functools.partial(along, p))
        update(p, lam0, keep_lam)
        start_v(1, p, lam1)

    for p in range(2):
        own(1, p, lam1)
        each_part(functools.partial(across, p))
    for p in range(2):
        beside(1, p, lam1)
        each_part(functools.partial(along, p))
        update(p, lam1, give)

    for k in range(1, n):
        main_copy(lax.rem(z + k, n)).wait_send()

    @pl.when(top)
    def _():
        far_up.wait_send()

    @pl.when(bottom)
    def _():
        far_down.wait_send()

    def drain(copies, ups, downs):
        up, down, left, right = copies

        @pl.when(ups)
        def _():
            up.wait_send()

        @pl.when(downs)
        def _():
            down.wait_send()

        left.wait_send()
        right.wait_send()

    each_part(lambda j: drain(halo_copies(j), gives_up, gives_down))
    for p in range(2):
        drain(v_copies(0, p, lam0), has_above, has_below)
        drain(v_copies(1, p, lam1), has_above, has_below)


def local(mesh_sizes, lam_start, adj_source, coef_points, quad_index, mode_index):
    n, ngx, ncore = mesh_sizes
    modes = lam_start.shape[0]
    points, inputs = quad_index.shape
    pts = coef_points.shape[0]
    rows_p = -(-modes // 16) * 16
    wide = -(-modes // 128) * 128
    dims = (n, ncore, ngx, inputs, modes, rows_p, wide, points, pts)

    hbm = pl.BlockSpec(memory_space=pltpu.HBM)
    dma = pltpu.SemaphoreType.DMA
    out = pl.pallas_call(
        functools.partial(kernel, dims),
        out_shape=jax.ShapeDtypeStruct((modes, 2, 128), f32),
        in_specs=[hbm] * 5,
        out_specs=pl.BlockSpec(memory_space=pltpu.VMEM),
        scratch_shapes=[
            pltpu.VMEM((modes, 2, 128), f32),
            pltpu.VMEM((modes, 2, 128), f32),
            pltpu.VMEM((inputs, points), jnp.int32),
            pltpu.VMEM((inputs, modes), jnp.int32),
            pltpu.VMEM((n, pts, 2, 128), f32),
            pltpu.VMEM((pts, 2, 128), f32),
            pltpu.VMEM((pts, 128), f32),
            pltpu.VMEM((n, 2, pts, 128), f32),
            pltpu.VMEM((n, 2, pts, 128), f32),
            pltpu.VMEM((n, 2, pts, 128), f32),
            pltpu.VMEM((n, 2, 2, 8, pts), f32),
            pltpu.VMEM((n, 2, 2, 8, pts), f32),
            pltpu.VMEM((2, rows_p, 128), f32),
            pltpu.VMEM((2, rows_p, 128), f32),
            pltpu.VMEM((STEPS, 2, 2, rows_p, 128), f32),
            pltpu.VMEM((STEPS, 2, 2, 8, wide), f32),
            pltpu.VMEM((STEPS, 2, 2, 8, wide), f32),
            pltpu.VMEM((2, 4, points, 128), f32),
            pltpu.VMEM((points, wide), bf16),
            pltpu.VMEM((points, wide), bf16),
            pltpu.VMEM((rows_p, points), bf16),
            pltpu.VMEM((rows_p, points), bf16),
            pltpu.VMEM((2, points, 128), bf16),
            pltpu.VMEM((2, points, 128), bf16),
            pltpu.VMEM((2, points, 128), f32),
            dma((6,)), dma((n,)), dma((n,)), dma, dma((2, n)), dma((2, n)), dma((2, n)), dma((2, n)),
            dma((STEPS, 4, 2)), dma((STEPS, 4, 2)),
        ],
        compiler_params=pltpu.CompilerParams(
            collective_id=0, has_side_effects=True, vmem_limit_bytes=40 * 1024 * 1024
        ),
    )(*[pltpu.with_memory_space_constraint(v, pltpu.HBM) for v in (lam_start, adj_source, coef_points, quad_index.T, mode_index.T)])
    return out


def solution(mesh):
    sizes = (mesh.shape["chaos"], mesh.shape["gx"], mesh.shape["gy"])
    placed = (
        P(None, ("chaos", "gy"), "gx"),
        P(None, ("chaos", "gy"), "gx"),
        P("chaos", None, "gy", "gx"),
        P(),
        P(),
    )
    return jax.shard_map(
        functools.partial(local, sizes),
        mesh=mesh,
        in_specs=placed,
        out_specs=P(None, ("chaos", "gy"), "gx"),
        check_vma=False,
    )
```

```python
import functools
import math

import jax
import jax.numpy as jnp
from jax import lax
from jax.experimental import pallas as pl
from jax.experimental.pallas import tpu as pltpu
from jax.sharding import PartitionSpec as P

STEPS = 2
FACTORS = 3

gauss_nodes = (-2.3344142183389773, -0.7419637843027259, 0.7419637843027259, 2.3344142183389773)
gauss_weights = (0.04587585476806849, 0.4541241452319315, 0.4541241452319315, 0.04587585476806849)
mass_shift = 1.0
relax_rate = 0.2
f32 = jnp.float32
bf16 = jnp.bfloat16


def split(x):
    high = x.astype(bf16)
    return high, (x - high.astype(f32)).astype(bf16)


dot = functools.partial(jnp.dot, preferred_element_type=f32)


def dot3(ah, al, bh, bl):
    return dot(ah, bh) + (dot(ah, bl) + dot(al, bh))


def kernel(
    dims, lam_hbm, adj_hbm, coef_hbm, quad_hbm, mode_hbm, out_ref,
    lam_raw, adj_ref, quad_ref, mode_ref, kraw, kall, kfar, kmid, khalo, kedge, ksend, krecv, kpack, kends,
    lam0, lam1, vhalo, vsend, vrecv, g_in, g_x, g_e, g_y, psi, bt_h, bt_l, v_cat,
    in_sem, main_send, main_recv, far_send, halo_send, halo_recv, edge_send, edge_recv, ends_send, ends_recv,
    v_send, v_recv,
):
    n, ncore, ngx, inputs, modes, rows_p, wide, points, pts = dims
    full = rows_p // 128 * 128
    tail = rows_p - full
    z, x, c = lax.axis_index("chaos"), lax.axis_index("gx"), lax.axis_index("gy")
    count = n * ncore
    me = z * ncore + c
    above = lax.rem(me + 1, count)
    below = lax.rem(me + count - 1, count)
    has_above, has_below = me < count - 1, me > 0
    dev_above = {"chaos": lax.div(above, ncore), "gy": lax.rem(above, ncore)}
    dev_below = {"chaos": lax.div(below, ncore), "gy": lax.rem(below, ncore)}
    dev_right = {"gx": lax.rem(x + 1, ngx)}
    dev_left = {"gx": lax.rem(x + ngx - 1, ngx)}
    half = n // 2
    top, bottom = c == ncore - 1, c == 0

    def gives_up(j):
        straight = (j == z + 1) | ((z + 1 == half) & (j > half))
        return has_above & jnp.logical_not(top & straight)

    def gives_down(j):
        straight = (j == z - 1) | ((z == half) & (j < half - 1))
        return has_below & jnp.logical_not(bottom & straight)

    def remote(src, dst, ss, rs, dev):
        return pltpu.make_async_remote_copy(
            src_ref=src, dst_ref=dst, send_sem=ss, recv_sem=rs, device_id=dev,
            device_id_type=pl.DeviceIdType.MESH,
        )

    def part_of(j):
        return pl.ds(pl.multiple_of(j * pts, pts), pts)

    get_own = pltpu.make_async_copy(coef_hbm.at[:, z], kraw.at[z], in_sem.at[0])
    get_all = pltpu.make_async_copy(coef_hbm, kall, in_sem.at[1])
    get_lam = pltpu.make_async_copy(lam_hbm, lam_raw, in_sem.at[2])
    get_quad = pltpu.make_async_copy(quad_hbm, quad_ref, in_sem.at[3])
    get_mode = pltpu.make_async_copy(mode_hbm, mode_ref, in_sem.at[4])
    get_adj = pltpu.make_async_copy(adj_hbm, adj_ref, in_sem.at[5])

    barrier = pltpu.get_barrier_semaphore()

    def greet(dev):
        pl.semaphore_signal(barrier, inc=1, device_id=dev, device_id_type=pl.DeviceIdType.MESH)

    def greet_line(i, carry):
        other = lax.rem(me + i, count)
        greet({"chaos": lax.div(other, ncore), "gy": lax.rem(other, ncore)})
        return carry

    lax.fori_loop(1, count, greet_line, 0, unroll=count <= 8)
    greet(dev_left)
    greet(dev_right)
    for get in (get_own, get_all, get_lam, get_quad, get_mode, get_adj):
        get.start()
    pl.semaphore_wait(barrier, count + 1)

    def main_copy(to):
        return remote(coef_hbm.at[:, to], kraw.at[z], main_send.at[to], main_recv.at[z], {"chaos": to})

    sign = 1 - 2 * lax.rem(z, 2)
    inner = (4 * z >= n) & (4 * z < 3 * n)
    outer_order = sorted(range(1, n), key=lambda k: (abs(2 * k - n), -k))
    inner_order = sorted(range(1, n), key=lambda k: (-abs(2 * k - n), k)) if n != 4 else [1, 2, 3]

    def partner(i):
        return lax.rem(z + n + sign * jnp.where(inner, inner_order[i], outer_order[i]), n)

    for i in range(n - 1):
        main_copy(partner(i)).start()

    def straight(slot, block, row, side, dev, cond):
        def copy():
            return remote(kfar.at[slot], khalo.at[side, part_of(z)], far_send.at[slot], halo_recv.at[side, z], dev)

        def start():
            @pl.when(cond)
            def _():
                kfar[slot] = kall[:, block, row, :]
                copy().start()

        def drain():
            @pl.when(cond)
            def _():
                copy().wait_send()

        return start, drain

    straights = (
        straight(0, lax.max(z - 1, 0), 1, 0, {"gy": 0}, top & (z > 0)),
        straight(1, lax.min(z + 1, n - 1), 0, 1, {"gy": ncore - 1}, bottom & (z < n - 1)),
        straight(2, half - 1, 1, 0, {"chaos": half, "gy": 0}, top & (z > half)),
        straight(3, half, 0, 1, {"chaos": half - 1, "gy": ncore - 1}, bottom & (z < half - 1)),
    )
    get_all.wait()
    for start, _ in straights:
        start()

    def v_copies(step, p, src):
        return (
            remote(src.at[p], vhalo.at[step, 0, p], v_send.at[step, 0, p], v_recv.at[step, 0, p], dev_above),
            remote(src.at[p], vhalo.at[step, 1, p], v_send.at[step, 1, p], v_recv.at[step, 1, p], dev_below),
            remote(vsend.at[step, 0, p], vrecv.at[step, 1, p], v_send.at[step, 2, p], v_recv.at[step, 2, p], dev_left),
            remote(vsend.at[step, 1, p], vrecv.at[step, 0, p], v_send.at[step, 3, p], v_recv.at[step, 3, p], dev_right),
        )

    def start_rows(step, p, src):
        up, down = v_copies(step, p, src)[:2]

        @pl.when(has_above)
        def _():
            up.start()

        @pl.when(has_below)
        def _():
            down.start()

    def start_edges(step, p, src):
        left, right = v_copies(step, p, src)[2:]
        flipped = jnp.concatenate([src[p], jnp.zeros((wide - rows_p, 128), f32)], 0).T
        vsend[step, 0, p] = flipped[:8]
        vsend[step, 1, p] = flipped[120:]
        left.start()
        right.start()

    def halo_copies(j):
        return (
            remote(kmid.at[1, part_of(j)], khalo.at[0, part_of(j)], halo_send.at[0, j], halo_recv.at[0, j], dev_above),
            remote(kmid.at[0, part_of(j)], khalo.at[1, part_of(j)], halo_send.at[1, j], halo_recv.at[1, j], dev_below),
        )

    def forward(j):
        up, down = halo_copies(j)
        for r in range(2):
            kmid[r, part_of(j), :] = kraw[j, :, r, :]

        @pl.when(gives_up(j))
        def _():
            up.start()

        @pl.when(gives_down(j))
        def _():
            down.start()

    edge_left = remote(ksend.at[0], krecv.at[1], edge_send.at[0], edge_recv.at[0], dev_left)
    edge_right = remote(ksend.at[1], krecv.at[0], edge_send.at[1], edge_recv.at[1], dev_right)

    def start_ends():
        for i in range(2 * n):
            flipped = kall[:, i // 2, i % 2, :].T
            ksend[0, i : i + 1] = flipped[:1]
            ksend[1, i : i + 1] = flipped[127:]
        edge_left.start()
        edge_right.start()

    def ends_copy(to):
        return remote(kpack.at[to], kends.at[z], ends_send.at[to], ends_recv.at[z], {"chaos": to})

    def pass_ends():
        edge_left.wait_recv()
        edge_right.wait_recv()
        for j in range(n):
            kpack[j, :2] = krecv[0, 2 * j : 2 * j + 2]
            kpack[j, 2:6] = jnp.zeros((4, pts), f32)
            kpack[j, 6:] = krecv[1, 2 * j : 2 * j + 2]
        kends[z] = kpack[z]
        for i in range(n - 1):
            ends_copy(partner(i)).start()

    get_lam.wait()
    for p in range(2):
        lam0[p, :modes] = lam_raw[:, p, :]
        lam0[p, modes:] = jnp.zeros((rows_p - modes, 128), f32)
    for p in range(2):
        start_edges(0, p, lam0)
    start_ends()
    get_own.wait()
    forward(z)

    v_cat[...] = jnp.zeros(v_cat.shape, bf16)

    @pl.when(jnp.logical_not(has_below))
    def _():
        khalo[0] = jnp.zeros((points, 128), f32)
        vhalo[:, 0] = jnp.zeros((STEPS, 2, rows_p, 128), f32)

    @pl.when(jnp.logical_not(has_above))
    def _():
        khalo[1] = jnp.zeros((points, 128), f32)
        vhalo[:, 1] = jnp.zeros((STEPS, 2, rows_p, 128), f32)

    def tables():
        get_quad.wait()
        get_mode.wait()
        quad = quad_ref[...]
        each = jnp.where((quad == 0) | (quad == 3), gauss_weights[0], gauss_weights[1]).astype(f32)
        wts = each[:1]
        for d in range(1, inputs):
            wts = wts * each[d : d + 1]
        wts = wts / jnp.sum(wts, axis=1, keepdims=True) * 0.25
        node = jnp.where(
            quad == 0, gauss_nodes[0],
            jnp.where(quad == 1, gauss_nodes[1], jnp.where(quad == 2, gauss_nodes[2], gauss_nodes[3])),
        ).astype(f32)
        h2 = (node * node - 1.0) * (1.0 / math.sqrt(2.0))
        h3 = (node * node * node - 3.0 * node) * (1.0 / math.sqrt(6.0))
        fill = jnp.zeros((16 - inputs, points), f32)
        one = jnp.ones((16, points), f32)
        table = jnp.concatenate([node, fill, h2, fill, h3, fill, one], 0)
        first = table.astype(bf16).astype(f32)
        rest = table - first
        second = rest.astype(bf16).astype(f32)
        third = rest - second
        pieces = jnp.concatenate([first, second, third, jnp.zeros((64, points), f32)], 0)
        by_point = pieces.T.astype(bf16)

        deg = jnp.concatenate([mode_ref[...], jnp.zeros((inputs, wide - modes), jnp.int32)], 1)
        run = jnp.zeros((1, wide), jnp.int32)
        runs = []
        for d in range(inputs):
            run = run + jnp.where(deg[d : d + 1] > 0, 1, 0)
            runs.append(run)
        nth = jnp.concatenate(runs, 0)
        blank = jnp.zeros((16 - inputs, wide), f32)
        real = lax.broadcasted_iota(jnp.int32, (1, wide), 1) < modes
        product = None
        for i in range(FACTORS):
            picks = []
            for k in range(1, 4):
                picks.append(jnp.where((deg == k) & (nth == i + 1), 1.0, 0.0).astype(f32))
                picks.append(blank)
            picks.append(jnp.where((run <= i) & real, 1.0, 0.0).astype(f32))
            picks.append(jnp.zeros((15, wide), f32))
            pick = jnp.concatenate(picks, 0)
            pick = jnp.concatenate([pick, pick, pick, jnp.zeros((64, wide), f32)], 0).astype(bf16)
            factor = jnp.dot(by_point, pick, preferred_element_type=f32)
            product = factor if product is None else product * factor
        high, low = split(product)
        psi[:, :full] = high[:, :full]
        psi[:, full : 2 * full] = low[:, :full]
        psi[:, 2 * full : 3 * full] = high[:, :full]
        if tail:
            high_end = high[:, full:].astype(f32)
            low_end = low[:, full:].astype(f32)
            psi[:, 3 * full :] = (
                high_end + pltpu.roll(low_end, tail, 1) + pltpu.roll(high_end, 2 * tail, 1)
            ).astype(bf16)
        for i in range(points // 128):
            part = slice(i * 128, i * 128 + 128)
            flipped = product[part].T[:rows_p] * wts[:, part]
            high, low = split(flipped)
            bt_h[:, part] = high
            bt_l[:, part] = low

    tables()

    lane = lax.broadcasted_iota(jnp.int32, (1, 128), 1)
    is_first, is_last = lane == 0, lane == 127
    ends = is_first | is_last

    def to_points(at, first, second):
        vh, vl = split(jnp.concatenate([first, second], 1))
        v_cat[at, :full] = vh[:full]
        v_cat[at, full : 2 * full] = vh[:full]
        v_cat[at, 2 * full : 3 * full] = vl[:full]
        if tail:
            v_cat[at, 3 * full : 3 * full + tail] = vh[full:]
            v_cat[at, 3 * full + tail : 3 * full + 2 * tail] = vh[full:]
            v_cat[at, 3 * full + 2 * tail : 3 * full + 3 * tail] = vl[full:]
        return dot(psi[...], v_cat[at])

    def step_over(v):
        return jnp.where(is_last, 0.0, pltpu.roll(v, 127, 1)) - jnp.where(is_first, 0.0, pltpu.roll(v, 1, 1))

    def own(src):
        g_in[...] = to_points(0, step_over(src[0]), step_over(src[1]))

    def own_ends(step, p, src):
        left, right = v_copies(step, p, src)[2:]
        left.wait_recv()
        right.wait_recv()
        gap = jnp.zeros((112, wide), f32)

        def columns(back):
            first, last = pltpu.roll(vrecv[step, 0, p], back, 0), pltpu.roll(vrecv[step, 1, p], 8 - back, 0)
            return jnp.concatenate([first, gap, last], 0).T[:rows_p]

        near, far = columns(1), columns(2)
        missing = jnp.where(is_first, -near, jnp.where(is_last, near, 0.0))
        beyond = jnp.where(ends, far - src[p], 0.0)
        got = to_points(1 + p, missing, beyond)
        g_x[p] = g_in[:, p * 128 : p * 128 + 128] + got[:, :128]
        g_e[p] = got[:, 128:]

    def beside(step, p, src):
        up, down = v_copies(step, p, src)[:2]

        @pl.when(has_below)
        def _():
            up.wait_recv()

        @pl.when(has_above)
        def _():
            down.wait_recv()

        mid = src[p]
        g_y[p] = to_points(3 + p, mid - vhalo[step, 0, p], vhalo[step, 1, p] - mid)

    def each_part(body):
        def step(j, carry):
            body(j)
            return carry

        lax.fori_loop(0, n, step, 0, unroll=n <= 4)

    def update(p, src, store):
        k_low = khalo[0] if p == 0 else kmid[0]
        k_high = kmid[1] if p == 0 else khalo[1]
        flux = kmid[p] * g_x[p]
        rest = k_high * g_y[p, :, 128:] - k_low * g_y[p, :, :128] + kedge[p] * g_e[p]
        high, low = split(jnp.concatenate([rest, flux], 1))
        back = dot3(bt_h[...], bt_l[...], high, low)
        div = back[:, :128] + step_over(back[:, 128:])
        v = src[p, :modes]
        store(p, v + relax_rate * (adj_ref[:, p, :] - (mass_shift * v - div[:modes])))

    def receive(j):
        remote(coef_hbm.at[:, j], kraw.at[j], main_send.at[j], main_recv.at[j], {"chaos": j}).wait_recv()
        forward(j)

    def arrive(j):
        found = kends[j]
        for p in range(2):
            first, last = (found, pltpu.roll(found, 1, 0)) if p == 0 else (pltpu.roll(found, 7, 0), found)
            kedge[p, part_of(j), :] = jnp.concatenate([first, jnp.zeros((112, pts), f32), last], 0).T

    def source(i):
        k = outer_order[-1 - i]
        return lax.rem(z + n + sign * (k if k % 2 else -k), n)

    order = [z] + [source(i) for i in range(n - 1)]
    own(lam0)
    pass_ends()
    for p in range(2):
        start_rows(0, p, lam0)
    for i in range(1, n):
        receive(order[i])
    for p in range(2):
        own_ends(0, p, lam0)
    for i in range(1, n):
        remote(kpack.at[order[i]], kends.at[order[i]], ends_send.at[order[i]], ends_recv.at[order[i]], {"chaos": order[i]}).wait_recv()
    for i in range(n):
        arrive(order[i])

    def halo_arrive(p):
        def body(j):
            up, down = halo_copies(j)
            if p == 0:
                @pl.when(has_below)
                def _():
                    up.wait_recv()
            else:
                @pl.when(has_above)
                def _():
                    down.wait_recv()

        each_part(body)

    def keep_lam(p, value):
        lam1[p, :modes] = value
        lam1[p, modes:] = jnp.zeros((rows_p - modes, 128), f32)

    def give(p, value):
        out_ref[:, p, :] = value

    get_adj.wait()
    for p in range(2):
        beside(0, p, lam0)
        halo_arrive(p)
        update(p, lam0, keep_lam)
        start_rows(1, p, lam1)
        start_edges(1, p, lam1)

    own(lam1)
    for p in range(2):
        own_ends(1, p, lam1)
        beside(1, p, lam1)
        update(p, lam1, give)

    for k in range(1, n):
        main_copy(lax.rem(z + k, n)).wait_send()
        ends_copy(lax.rem(z + k, n)).wait_send()
    edge_left.wait_send()
    edge_right.wait_send()

    for _, finish in straights:
        finish()

    def drain(copies, ups, downs):
        @pl.when(ups)
        def _():
            copies[0].wait_send()

        @pl.when(downs)
        def _():
            copies[1].wait_send()

        for copy in copies[2:]:
            copy.wait_send()

    each_part(lambda j: drain(halo_copies(j), gives_up(j), gives_down(j)))
    for p in range(2):
        drain(v_copies(0, p, lam0), has_above, has_below)
        drain(v_copies(1, p, lam1), has_above, has_below)


def local(mesh_sizes, lam_start, adj_source, coef_points, quad_index, mode_index):
    n, ngx, ncore = mesh_sizes
    modes = lam_start.shape[0]
    points, inputs = quad_index.shape
    pts = coef_points.shape[0]
    rows_p = -(-modes // 16) * 16
    wide = -(-modes // 128) * 128
    depth = -(-3 * rows_p // 128) * 128
    dims = (n, ncore, ngx, inputs, modes, rows_p, wide, points, pts)

    hbm = pl.BlockSpec(memory_space=pltpu.HBM)
    dma = pltpu.SemaphoreType.DMA
    out = pl.pallas_call(
        functools.partial(kernel, dims),
        out_shape=jax.ShapeDtypeStruct((modes, 2, 128), f32),
        in_specs=[hbm] * 5,
        out_specs=pl.BlockSpec(memory_space=pltpu.VMEM),
        scratch_shapes=[
            pltpu.VMEM((modes, 2, 128), f32),
            pltpu.VMEM((modes, 2, 128), f32),
            pltpu.VMEM((inputs, points), jnp.int32),
            pltpu.VMEM((inputs, modes), jnp.int32),
            pltpu.VMEM((n, pts, 2, 128), f32),
            pltpu.VMEM((pts, n, 2, 128), f32),
            pltpu.VMEM((4, pts, 128), f32),
            pltpu.VMEM((2, points, 128), f32),
            pltpu.VMEM((2, points, 128), f32),
            pltpu.VMEM((2, points, 128), f32),
            pltpu.VMEM((2, 2 * n, pts), f32),
            pltpu.VMEM((2, 2 * n, pts), f32),
            pltpu.VMEM((n, 8, pts), f32),
            pltpu.VMEM((n, 8, pts), f32),
            pltpu.VMEM((2, rows_p, 128), f32),
            pltpu.VMEM((2, rows_p, 128), f32),
            pltpu.VMEM((STEPS, 2, 2, rows_p, 128), f32),
            pltpu.VMEM((STEPS, 2, 2, 8, wide), f32),
            pltpu.VMEM((STEPS, 2, 2, 8, wide), f32),
            pltpu.VMEM((points, 256), f32),
            pltpu.VMEM((2, points, 128), f32),
            pltpu.VMEM((2, points, 128), f32),
            pltpu.VMEM((2, points, 256), f32),
            pltpu.VMEM((points, depth), bf16),
            pltpu.VMEM((rows_p, points), bf16),
            pltpu.VMEM((rows_p, points), bf16),
            pltpu.VMEM((5, depth, 256), bf16),
            dma((6,)), dma((n,)), dma((n,)), dma((4,)), dma((2, n)), dma((2, n)), dma((2,)), dma((2,)), dma((n,)), dma((n,)),
            dma((STEPS, 4, 2)), dma((STEPS, 4, 2)),
        ],
        compiler_params=pltpu.CompilerParams(
            collective_id=0, has_side_effects=True, vmem_limit_bytes=40 * 1024 * 1024
        ),
    )(*[pltpu.with_memory_space_constraint(v, pltpu.HBM) for v in (lam_start, adj_source, coef_points, quad_index.T, mode_index.T)])
    return out


def solution(mesh):
    sizes = (mesh.shape["chaos"], mesh.shape["gx"], mesh.shape["gy"])
    placed = (
        P(None, ("chaos", "gy"), "gx"),
        P(None, ("chaos", "gy"), "gx"),
        P("chaos", None, "gy", "gx"),
        P(),
        P(),
    )
    return jax.shard_map(
        functools.partial(local, sizes),
        mesh=mesh,
        in_specs=placed,
        out_specs=P(None, ("chaos", "gy"), "gx"),
        check_vma=False,
    )
```

```python
import functools
import math

import jax
import jax.numpy as jnp
from jax import lax
from jax.experimental import pallas as pl
from jax.experimental.pallas import tpu as pltpu
from jax.sharding import PartitionSpec as P

STEPS = 2
FACTORS = 3

gauss_nodes = (-2.3344142183389773, -0.7419637843027259, 0.7419637843027259, 2.3344142183389773)
gauss_weights = (0.04587585476806849, 0.4541241452319315, 0.4541241452319315, 0.04587585476806849)
mass_shift = 1.0
relax_rate = 0.2
f32 = jnp.float32
bf16 = jnp.bfloat16


def split(x):
    high = x.astype(bf16)
    return high, (x - high.astype(f32)).astype(bf16)


dot = functools.partial(jnp.dot, preferred_element_type=f32)


def dot3(ah, al, bh, bl):
    return dot(ah, bh) + (dot(ah, bl) + dot(al, bh))


def kernel(
    dims, lam_hbm, adj_hbm, coef_hbm, quad_hbm, mode_hbm, out_ref,
    lam_raw, adj_ref, quad_ref, mode_ref, kraw, kall, kfar, kmid, khalo, kedge, ksend, krecv, kpack, kends,
    lam0, lam1, vhalo, vsend, vrecv, g_in, g_x, g_e, g_y, psi, bt_h, bt_l, v_cat, e_cat,
    in_sem, main_send, main_recv, far_send, halo_send, halo_recv, edge_send, edge_recv, ends_send, ends_recv,
    v_send, v_recv,
):
    n, ncore, ngx, inputs, modes, rows_p, wide, points, pts = dims
    full = rows_p // 128 * 128
    tail = rows_p - full
    z, x, c = lax.axis_index("chaos"), lax.axis_index("gx"), lax.axis_index("gy")
    count = n * ncore
    me = z * ncore + c
    above = lax.rem(me + 1, count)
    below = lax.rem(me + count - 1, count)
    has_above, has_below = me < count - 1, me > 0
    dev_above = {"chaos": lax.div(above, ncore), "gy": lax.rem(above, ncore)}
    dev_below = {"chaos": lax.div(below, ncore), "gy": lax.rem(below, ncore)}
    dev_right = {"gx": lax.rem(x + 1, ngx)}
    dev_left = {"gx": lax.rem(x + ngx - 1, ngx)}
    half = n // 2
    top, bottom = c == ncore - 1, c == 0

    def gives_up(j):
        straight = (j == z + 1) | ((z + 1 == half) & (j > half))
        return has_above & jnp.logical_not(top & straight)

    def gives_down(j):
        straight = (j == z - 1) | ((z == half) & (j < half - 1))
        return has_below & jnp.logical_not(bottom & straight)

    def remote(src, dst, ss, rs, dev):
        return pltpu.make_async_remote_copy(
            src_ref=src, dst_ref=dst, send_sem=ss, recv_sem=rs, device_id=dev,
            device_id_type=pl.DeviceIdType.MESH,
        )

    def part_of(j):
        return pl.ds(pl.multiple_of(j * pts, pts), pts)

    get_own = pltpu.make_async_copy(coef_hbm.at[:, z], kraw.at[z], in_sem.at[0])
    get_all = pltpu.make_async_copy(coef_hbm, kall, in_sem.at[1])
    get_lam = pltpu.make_async_copy(lam_hbm, lam_raw, in_sem.at[2])
    get_quad = pltpu.make_async_copy(quad_hbm, quad_ref, in_sem.at[3])
    get_mode = pltpu.make_async_copy(mode_hbm, mode_ref, in_sem.at[4])
    get_adj = pltpu.make_async_copy(adj_hbm, adj_ref, in_sem.at[5])

    barrier = pltpu.get_barrier_semaphore()

    def greet(dev):
        pl.semaphore_signal(barrier, inc=1, device_id=dev, device_id_type=pl.DeviceIdType.MESH)

    def greet_line(i, carry):
        other = lax.rem(me + i, count)
        greet({"chaos": lax.div(other, ncore), "gy": lax.rem(other, ncore)})
        return carry

    lax.fori_loop(1, count, greet_line, 0, unroll=count <= 8)
    greet(dev_left)
    greet(dev_right)
    for get in (get_own, get_all, get_lam, get_quad, get_mode, get_adj):
        get.start()
    pl.semaphore_wait(barrier, count + 1)

    def main_copy(to):
        return remote(coef_hbm.at[:, to], kraw.at[z], main_send.at[to], main_recv.at[z], {"chaos": to})

    sign = 1 - 2 * lax.rem(z, 2)
    inner = (4 * z >= n) & (4 * z < 3 * n)
    outer_order = sorted(range(1, n), key=lambda k: (abs(2 * k - n), -k))
    inner_order = sorted(range(1, n), key=lambda k: (-abs(2 * k - n), k)) if n != 4 else [1, 2, 3]

    def partner(i):
        return lax.rem(z + n + sign * jnp.where(inner, inner_order[i], outer_order[i]), n)

    for i in range(n - 1):
        main_copy(partner(i)).start()

    def straight(slot, block, row, side, dev, cond):
        def copy():
            return remote(kfar.at[slot], khalo.at[side, part_of(z)], far_send.at[slot], halo_recv.at[side, z], dev)

        def start():
            @pl.when(cond)
            def _():
                kfar[slot] = kall[:, block, row, :]
                copy().start()

        def drain():
            @pl.when(cond)
            def _():
                copy().wait_send()

        return start, drain

    straights = (
        straight(0, lax.max(z - 1, 0), 1, 0, {"gy": 0}, top & (z > 0)),
        straight(1, lax.min(z + 1, n - 1), 0, 1, {"gy": ncore - 1}, bottom & (z < n - 1)),
        straight(2, half - 1, 1, 0, {"chaos": half, "gy": 0}, top & (z > half)),
        straight(3, half, 0, 1, {"chaos": half - 1, "gy": ncore - 1}, bottom & (z < half - 1)),
    )
    get_all.wait()
    for start, _ in straights:
        start()

    def v_copies(step, p, src):
        return (
            remote(src.at[p], vhalo.at[step, 0, p], v_send.at[step, 0, p], v_recv.at[step, 0, p], dev_above),
            remote(src.at[p], vhalo.at[step, 1, p], v_send.at[step, 1, p], v_recv.at[step, 1, p], dev_below),
            remote(vsend.at[step, 0, p], vrecv.at[step, 1, p], v_send.at[step, 2, p], v_recv.at[step, 2, p], dev_left),
            remote(vsend.at[step, 1, p], vrecv.at[step, 0, p], v_send.at[step, 3, p], v_recv.at[step, 3, p], dev_right),
        )

    def start_rows(step, p, src):
        up, down = v_copies(step, p, src)[:2]

        @pl.when(has_above)
        def _():
            up.start()

        @pl.when(has_below)
        def _():
            down.start()

    def start_edges(step, p, src):
        left, right = v_copies(step, p, src)[2:]
        flipped = jnp.concatenate([src[p], jnp.zeros((wide - rows_p, 128), f32)], 0).T
        vsend[step, 0, p] = flipped[:8]
        vsend[step, 1, p] = flipped[120:]
        left.start()
        right.start()

    def halo_copies(j):
        return (
            remote(kmid.at[1, part_of(j)], khalo.at[0, part_of(j)], halo_send.at[0, j], halo_recv.at[0, j], dev_above),
            remote(kmid.at[0, part_of(j)], khalo.at[1, part_of(j)], halo_send.at[1, j], halo_recv.at[1, j], dev_below),
        )

    def forward(j):
        up, down = halo_copies(j)
        for r in range(2):
            kmid[r, part_of(j), :] = kraw[j, :, r, :]

        @pl.when(gives_up(j))
        def _():
            up.start()

        @pl.when(gives_down(j))
        def _():
            down.start()

    edge_left = remote(ksend.at[0], krecv.at[1], edge_send.at[0], edge_recv.at[0], dev_left)
    edge_right = remote(ksend.at[1], krecv.at[0], edge_send.at[1], edge_recv.at[1], dev_right)

    def start_ends():
        for i in range(2 * n):
            flipped = kall[:, i // 2, i % 2, :].T
            ksend[0, i : i + 1] = flipped[:1]
            ksend[1, i : i + 1] = flipped[127:]
        edge_left.start()
        edge_right.start()

    def ends_copy(to):
        return remote(kpack.at[to], kends.at[z], ends_send.at[to], ends_recv.at[z], {"chaos": to})

    def pass_ends():
        edge_left.wait_recv()
        edge_right.wait_recv()
        for j in range(n):
            kpack[j, :2] = krecv[0, 2 * j : 2 * j + 2]
            kpack[j, 2:6] = jnp.zeros((4, pts), f32)
            kpack[j, 6:] = krecv[1, 2 * j : 2 * j + 2]
        kends[z] = kpack[z]
        for i in range(n - 1):
            ends_copy(partner(i)).start()

    get_lam.wait()
    for p in range(2):
        lam0[p, :modes] = lam_raw[:, p, :]
        lam0[p, modes:] = jnp.zeros((rows_p - modes, 128), f32)
    for p in range(2):
        start_edges(0, p, lam0)
    start_ends()
    get_own.wait()
    forward(z)

    v_cat[...] = jnp.zeros(v_cat.shape, bf16)
    e_cat[...] = jnp.zeros(e_cat.shape, bf16)

    @pl.when(jnp.logical_not(has_below))
    def _():
        khalo[0] = jnp.zeros((points, 128), f32)
        vhalo[:, 0] = jnp.zeros((STEPS, 2, rows_p, 128), f32)

    @pl.when(jnp.logical_not(has_above))
    def _():
        khalo[1] = jnp.zeros((points, 128), f32)
        vhalo[:, 1] = jnp.zeros((STEPS, 2, rows_p, 128), f32)

    def tables():
        get_quad.wait()
        get_mode.wait()
        quad = quad_ref[...]
        each = jnp.where((quad == 0) | (quad == 3), gauss_weights[0], gauss_weights[1]).astype(f32)
        wts = each[:1]
        for d in range(1, inputs):
            wts = wts * each[d : d + 1]
        wts = wts / jnp.sum(wts, axis=1, keepdims=True) * 0.25
        node = jnp.where(
            quad == 0, gauss_nodes[0],
            jnp.where(quad == 1, gauss_nodes[1], jnp.where(quad == 2, gauss_nodes[2], gauss_nodes[3])),
        ).astype(f32)
        h2 = (node * node - 1.0) * (1.0 / math.sqrt(2.0))
        h3 = (node * node * node - 3.0 * node) * (1.0 / math.sqrt(6.0))
        fill = jnp.zeros((16 - inputs, points), f32)
        one = jnp.ones((16, points), f32)
        table = jnp.concatenate([node, fill, h2, fill, h3, fill, one], 0)
        first = table.astype(bf16).astype(f32)
        rest = table - first
        second = rest.astype(bf16).astype(f32)
        third = rest - second
        pieces = jnp.concatenate([first, second, third, jnp.zeros((64, points), f32)], 0)
        by_point = pieces.T.astype(bf16)

        deg = jnp.concatenate([mode_ref[...], jnp.zeros((inputs, wide - modes), jnp.int32)], 1)
        run = jnp.zeros((1, wide), jnp.int32)
        runs = []
        for d in range(inputs):
            run = run + jnp.where(deg[d : d + 1] > 0, 1, 0)
            runs.append(run)
        nth = jnp.concatenate(runs, 0)
        blank = jnp.zeros((16 - inputs, wide), f32)
        real = lax.broadcasted_iota(jnp.int32, (1, wide), 1) < modes
        product = None
        for i in range(FACTORS):
            picks = []
            for k in range(1, 4):
                picks.append(jnp.where((deg == k) & (nth == i + 1), 1.0, 0.0).astype(f32))
                picks.append(blank)
            picks.append(jnp.where((run <= i) & real, 1.0, 0.0).astype(f32))
            picks.append(jnp.zeros((15, wide), f32))
            pick = jnp.concatenate(picks, 0)
            pick = jnp.concatenate([pick, pick, pick, jnp.zeros((64, wide), f32)], 0).astype(bf16)
            factor = jnp.dot(by_point, pick, preferred_element_type=f32)
            product = factor if product is None else product * factor
        high, low = split(product)
        psi[:, :full] = high[:, :full]
        psi[:, full : 2 * full] = low[:, :full]
        psi[:, 2 * full : 3 * full] = high[:, :full]
        if tail:
            high_end = high[:, full:].astype(f32)
            low_end = low[:, full:].astype(f32)
            psi[:, 3 * full :] = (
                high_end + pltpu.roll(low_end, tail, 1) + pltpu.roll(high_end, 2 * tail, 1)
            ).astype(bf16)
        for i in range(points // 128):
            part = slice(i * 128, i * 128 + 128)
            flipped = product[part].T[:rows_p] * wts[:, part]
            high, low = split(flipped)
            bt_h[:, part] = high
            bt_l[:, part] = low

    tables()

    lane = lax.broadcasted_iota(jnp.int32, (1, 128), 1)
    is_first, is_last = lane == 0, lane == 127
    ends = is_first | is_last

    def to_points(at, first, second):
        vh, vl = split(jnp.concatenate([first, second], 1))
        v_cat[at, :full] = vh[:full]
        v_cat[at, full : 2 * full] = vh[:full]
        v_cat[at, 2 * full : 3 * full] = vl[:full]
        if tail:
            v_cat[at, 3 * full : 3 * full + tail] = vh[full:]
            v_cat[at, 3 * full + tail : 3 * full + 2 * tail] = vh[full:]
            v_cat[at, 3 * full + 2 * tail : 3 * full + 3 * tail] = vl[full:]
        return dot(psi[...], v_cat[at])

    def step_over(v):
        return jnp.where(is_last, 0.0, pltpu.roll(v, 127, 1)) - jnp.where(is_first, 0.0, pltpu.roll(v, 1, 1))

    def own(src):
        g_in[...] = to_points(0, step_over(src[0]), step_over(src[1]))

    def wait_sides(step, p, src):
        left, right = v_copies(step, p, src)[2:]
        left.wait_recv()
        right.wait_recv()

    def wait_rows(step, p, src):
        up, down = v_copies(step, p, src)[:2]

        @pl.when(has_below)
        def _():
            up.wait_recv()

        @pl.when(has_above)
        def _():
            down.wait_recv()

    def own_ends(step, p):
        def stacked(tile):
            high, low = split(tile)
            parts = [high[:, :full], high[:, :full], low[:, :full]]
            if tail:
                high_end = high[:, full:].astype(f32)
                low_end = low[:, full:].astype(f32)
                end = high_end + pltpu.roll(high_end, tail, 1) + pltpu.roll(low_end, 2 * tail, 1)
                parts.append(end.astype(bf16))
            return jnp.concatenate(parts, 1)

        row = lax.broadcasted_iota(jnp.int32, (8, wide), 0)
        none = jnp.zeros((8, wide), f32)
        from_left, from_right = vrecv[step, 0, p], vrecv[step, 1, p]
        first, last = vsend[step, 0, p], vsend[step, 1, p]
        near = jnp.where(row == 0, -pltpu.roll(from_left, 1, 0), 0.0)
        far = jnp.where(row == 0, pltpu.roll(from_left, 2, 0) - first, 0.0)
        e_cat[p, :16] = stacked(jnp.concatenate([near, none], 0))
        e_cat[p, 128:144] = stacked(jnp.concatenate([far, none], 0))
        near = jnp.where(row == 7, pltpu.roll(from_right, 7, 0), 0.0)
        far = jnp.where(row == 7, pltpu.roll(from_right, 6, 0) - last, 0.0)
        e_cat[p, 112:128] = stacked(jnp.concatenate([none, near], 0))
        e_cat[p, 240:] = stacked(jnp.concatenate([none, far], 0))
        got = lax.dot_general(psi[...], e_cat[p], (((1,), (1,)), ((), ())), preferred_element_type=f32)
        g_x[p] = g_in[:, p * 128 : p * 128 + 128] + got[:, :128]
        g_e[p] = got[:, 128:]

    def beside(step, p, src):
        mid = src[p]
        g_y[p] = to_points(1 + p, mid - vhalo[step, 0, p], vhalo[step, 1, p] - mid)

    def each_part(body):
        def step(j, carry):
            body(j)
            return carry

        lax.fori_loop(0, n, step, 0, unroll=n <= 4)

    def update(p, src, store):
        k_low = khalo[0] if p == 0 else kmid[0]
        k_high = kmid[1] if p == 0 else khalo[1]
        flux = kmid[p] * g_x[p]
        rest = k_high * g_y[p, :, 128:] - k_low * g_y[p, :, :128] + kedge[p] * g_e[p]
        high, low = split(jnp.concatenate([rest, flux], 1))
        back = dot3(bt_h[...], bt_l[...], high, low)
        div = back[:, :128] + step_over(back[:, 128:])
        v = src[p, :modes]
        store(p, v + relax_rate * (adj_ref[:, p, :] - (mass_shift * v - div[:modes])))

    def receive(j):
        remote(coef_hbm.at[:, j], kraw.at[j], main_send.at[j], main_recv.at[j], {"chaos": j}).wait_recv()
        forward(j)

    def arrive(j):
        found = kends[j]
        for p in range(2):
            first, last = (found, pltpu.roll(found, 1, 0)) if p == 0 else (pltpu.roll(found, 7, 0), found)
            kedge[p, part_of(j), :] = jnp.concatenate([first, jnp.zeros((112, pts), f32), last], 0).T

    def source(i):
        k = outer_order[-1 - i]
        return lax.rem(z + n + sign * (k if k % 2 else -k), n)

    order = [z] + [source(i) for i in range(n - 1)]
    own(lam0)
    pass_ends()
    start_rows(0, 0, lam0)
    for p in range(2):
        wait_sides(0, p, lam0)
    for p in range(2):
        own_ends(0, p)
    for i in range(1, 2):
        receive(order[i])
    start_rows(0, 1, lam0)
    for i in range(2, n):
        receive(order[i])
    for k in range(1, n):
        main_copy(lax.rem(z + k, n)).wait_send()
        ends_copy(lax.rem(z + k, n)).wait_send()
    edge_left.wait_send()
    edge_right.wait_send()

    for _, finish in straights:
        finish()

    def drain(copies, ups, downs):
        @pl.when(ups)
        def _():
            copies[0].wait_send()

        @pl.when(downs)
        def _():
            copies[1].wait_send()

        for copy in copies[2:]:
            copy.wait_send()

    for i in range(1, n):
        remote(kpack.at[order[i]], kends.at[order[i]], ends_send.at[order[i]], ends_recv.at[order[i]], {"chaos": order[i]}).wait_recv()
    for i in range(n):
        arrive(order[i])

    def halo_arrive(p):
        def body(j):
            up, down = halo_copies(j)
            if p == 0:
                @pl.when(has_below)
                def _():
                    up.wait_recv()
            else:
                @pl.when(has_above)
                def _():
                    down.wait_recv()

        each_part(body)

    def keep_lam(p, value):
        lam1[p, :modes] = value
        lam1[p, modes:] = jnp.zeros((rows_p - modes, 128), f32)

    def give(p, value):
        out_ref[:, p, :] = value

    get_adj.wait()
    for p in range(2):
        wait_rows(0, p, lam0)
        if p == 0:
            beside(0, p, lam0)
        halo_arrive(p)
        if p:
            beside(0, p, lam0)
        update(p, lam0, keep_lam)
        start_rows(1, p, lam1)
        start_edges(1, p, lam1)

    own(lam1)
    each_part(lambda j: drain(halo_copies(j), gives_up(j), gives_down(j)))
    for p in range(2):
        drain(v_copies(0, p, lam0), has_above, has_below)
    wait_sides(1, 0, lam1)
    wait_rows(1, 0, lam1)
    own_ends(1, 0)
    beside(1, 0, lam1)
    update(0, lam1, give)
    wait_sides(1, 1, lam1)
    wait_rows(1, 1, lam1)
    own_ends(1, 1)
    beside(1, 1, lam1)
    update(1, lam1, give)

    for p in range(2):
        drain(v_copies(1, p, lam1), has_above, has_below)


def local(mesh_sizes, lam_start, adj_source, coef_points, quad_index, mode_index):
    n, ngx, ncore = mesh_sizes
    modes = lam_start.shape[0]
    points, inputs = quad_index.shape
    pts = coef_points.shape[0]
    rows_p = -(-modes // 16) * 16
    wide = -(-modes // 128) * 128
    depth = -(-3 * rows_p // 128) * 128
    dims = (n, ncore, ngx, inputs, modes, rows_p, wide, points, pts)

    hbm = pl.BlockSpec(memory_space=pltpu.HBM)
    dma = pltpu.SemaphoreType.DMA
    out = pl.pallas_call(
        functools.partial(kernel, dims),
        out_shape=jax.ShapeDtypeStruct((modes, 2, 128), f32),
        in_specs=[hbm] * 5,
        out_specs=pl.BlockSpec(memory_space=pltpu.VMEM),
        scratch_shapes=[
            pltpu.VMEM((modes, 2, 128), f32),
            pltpu.VMEM((modes, 2, 128), f32),
            pltpu.VMEM((inputs, points), jnp.int32),
            pltpu.VMEM((inputs, modes), jnp.int32),
            pltpu.VMEM((n, pts, 2, 128), f32),
            pltpu.VMEM((pts, n, 2, 128), f32),
            pltpu.VMEM((4, pts, 128), f32),
            pltpu.VMEM((2, points, 128), f32),
            pltpu.VMEM((2, points, 128), f32),
            pltpu.VMEM((2, points, 128), f32),
            pltpu.VMEM((2, 2 * n, pts), f32),
            pltpu.VMEM((2, 2 * n, pts), f32),
            pltpu.VMEM((n, 8, pts), f32),
            pltpu.VMEM((n, 8, pts), f32),
            pltpu.VMEM((2, rows_p, 128), f32),
            pltpu.VMEM((2, rows_p, 128), f32),
            pltpu.VMEM((STEPS, 2, 2, rows_p, 128), f32),
            pltpu.VMEM((STEPS, 2, 2, 8, wide), f32),
            pltpu.VMEM((STEPS, 2, 2, 8, wide), f32),
            pltpu.VMEM((points, 256), f32),
            pltpu.VMEM((2, points, 128), f32),
            pltpu.VMEM((2, points, 128), f32),
            pltpu.VMEM((2, points, 256), f32),
            pltpu.VMEM((points, depth), bf16),
            pltpu.VMEM((rows_p, points), bf16),
            pltpu.VMEM((rows_p, points), bf16),
            pltpu.VMEM((3, depth, 256), bf16),
            pltpu.VMEM((2, 256, depth), bf16),
            dma((6,)), dma((n,)), dma((n,)), dma((4,)), dma((2, n)), dma((2, n)), dma((2,)), dma((2,)), dma((n,)), dma((n,)),
            dma((STEPS, 4, 2)), dma((STEPS, 4, 2)),
        ],
        compiler_params=pltpu.CompilerParams(
            collective_id=0, has_side_effects=True, vmem_limit_bytes=40 * 1024 * 1024
        ),
    )(*[pltpu.with_memory_space_constraint(v, pltpu.HBM) for v in (lam_start, adj_source, coef_points, quad_index.T, mode_index.T)])
    return out


def solution(mesh):
    sizes = (mesh.shape["chaos"], mesh.shape["gx"], mesh.shape["gy"])
    placed = (
        P(None, ("chaos", "gy"), "gx"),
        P(None, ("chaos", "gy"), "gx"),
        P("chaos", None, "gy", "gx"),
        P(),
        P(),
    )
    return jax.shard_map(
        functools.partial(local, sizes),
        mesh=mesh,
        in_specs=placed,
        out_specs=P(None, ("chaos", "gy"), "gx"),
        check_vma=False,
    )
```

```python
import functools
import math

import jax
import jax.numpy as jnp
from jax import lax
from jax.experimental import pallas as pl
from jax.experimental.pallas import tpu as pltpu
from jax.sharding import PartitionSpec as P

STEPS = 2
FACTORS = 3

gauss_nodes = (-2.3344142183389773, -0.7419637843027259, 0.7419637843027259, 2.3344142183389773)
gauss_weights = (0.04587585476806849, 0.4541241452319315, 0.4541241452319315, 0.04587585476806849)
mass_shift = 1.0
relax_rate = 0.2
f32 = jnp.float32
bf16 = jnp.bfloat16


def split(x):
    high = x.astype(bf16)
    return high, (x - high.astype(f32)).astype(bf16)


dot = functools.partial(jnp.dot, preferred_element_type=f32)


def dot3(ah, al, bh, bl):
    return dot(ah, bh) + (dot(ah, bl) + dot(al, bh))


def kernel(
    dims, lam_hbm, adj_hbm, coef_hbm, quad_hbm, mode_hbm, out_ref,
    lam_raw, adj_ref, quad_ref, mode_ref, kraw, kall, kfar, kmid, khalo, kedge, ksend, krecv, kpack, kends,
    lam0, lam1, vhalo, vsend, vrecv, g_in, g_x, g_e, g_y, psi, bt_h, bt_l, v_cat, e_cat,
    in_sem, main_send, main_recv, far_send, halo_send, halo_recv, edge_send, edge_recv, ends_send, ends_recv,
    v_send, v_recv,
):
    n, ncore, ngx, inputs, modes, rows_p, wide, points, pts = dims
    full = rows_p // 128 * 128
    tail = rows_p - full
    z, x, c = lax.axis_index("chaos"), lax.axis_index("gx"), lax.axis_index("gy")
    count = n * ncore
    me = z * ncore + c
    above = lax.rem(me + 1, count)
    below = lax.rem(me + count - 1, count)
    has_above, has_below = me < count - 1, me > 0
    dev_above = {"chaos": lax.div(above, ncore), "gy": lax.rem(above, ncore)}
    dev_below = {"chaos": lax.div(below, ncore), "gy": lax.rem(below, ncore)}
    dev_right = {"gx": lax.rem(x + 1, ngx)}
    dev_left = {"gx": lax.rem(x + ngx - 1, ngx)}
    half = n // 2
    top, bottom = c == ncore - 1, c == 0

    def gives_up(j):
        straight = (j == z + 1) | ((z + 1 == half) & (j > half))
        return has_above & jnp.logical_not(top & straight)

    def gives_down(j):
        straight = (j == z - 1) | ((z == half) & (j < half - 1))
        return has_below & jnp.logical_not(bottom & straight)

    def remote(src, dst, ss, rs, dev):
        return pltpu.make_async_remote_copy(
            src_ref=src, dst_ref=dst, send_sem=ss, recv_sem=rs, device_id=dev,
            device_id_type=pl.DeviceIdType.MESH,
        )

    def part_of(j):
        return pl.ds(pl.multiple_of(j * pts, pts), pts)

    get_own = pltpu.make_async_copy(coef_hbm.at[:, z], kraw.at[z], in_sem.at[0])
    get_all = pltpu.make_async_copy(coef_hbm, kall, in_sem.at[1])
    get_lam = pltpu.make_async_copy(lam_hbm, lam_raw, in_sem.at[2])
    get_quad = pltpu.make_async_copy(quad_hbm, quad_ref, in_sem.at[3])
    get_mode = pltpu.make_async_copy(mode_hbm, mode_ref, in_sem.at[4])
    get_adj = pltpu.make_async_copy(adj_hbm, adj_ref, in_sem.at[5])

    barrier = pltpu.get_barrier_semaphore()

    def greet(dev):
        pl.semaphore_signal(barrier, inc=1, device_id=dev, device_id_type=pl.DeviceIdType.MESH)

    def greet_line(i, carry):
        other = lax.rem(me + i, count)
        greet({"chaos": lax.div(other, ncore), "gy": lax.rem(other, ncore)})
        return carry

    lax.fori_loop(1, count, greet_line, 0, unroll=count <= 8)
    greet(dev_left)
    greet(dev_right)
    for get in (get_own, get_all, get_lam, get_quad, get_mode, get_adj):
        get.start()
    pl.semaphore_wait(barrier, count + 1)

    def main_copy(to):
        return remote(coef_hbm.at[:, to], kraw.at[z], main_send.at[to], main_recv.at[z], {"chaos": to})

    sign = 1 - 2 * lax.rem(z, 2)
    inner = (4 * z >= n) & (4 * z < 3 * n)
    outer_order = sorted(range(1, n), key=lambda k: (abs(2 * k - n), -k))
    inner_order = sorted(range(1, n), key=lambda k: (-abs(2 * k - n), k)) if n != 4 else [1, 2, 3]

    def partner(i):
        return lax.rem(z + n + sign * jnp.where(inner, inner_order[i], outer_order[i]), n)

    for i in range(n - 1):
        main_copy(partner(i)).start()

    def straight(slot, block, row, side, dev, cond):
        def copy():
            return remote(kfar.at[slot], khalo.at[side, part_of(z)], far_send.at[slot], halo_recv.at[side, z], dev)

        def start():
            @pl.when(cond)
            def _():
                kfar[slot] = kall[:, block, row, :]
                copy().start()

        def drain():
            @pl.when(cond)
            def _():
                copy().wait_send()

        return start, drain

    straights = (
        straight(0, lax.max(z - 1, 0), 1, 0, {"gy": 0}, top & (z > 0)),
        straight(1, lax.min(z + 1, n - 1), 0, 1, {"gy": ncore - 1}, bottom & (z < n - 1)),
        straight(2, half - 1, 1, 0, {"chaos": half, "gy": 0}, top & (z > half)),
        straight(3, half, 0, 1, {"chaos": half - 1, "gy": ncore - 1}, bottom & (z < half - 1)),
    )
    get_all.wait()
    for start, _ in straights:
        start()

    def v_copies(step, p, src):
        return (
            remote(src.at[p], vhalo.at[step, 0, p], v_send.at[step, 0, p], v_recv.at[step, 0, p], dev_above),
            remote(src.at[p], vhalo.at[step, 1, p], v_send.at[step, 1, p], v_recv.at[step, 1, p], dev_below),
            remote(vsend.at[step, 0, p], vrecv.at[step, 1, p], v_send.at[step, 2, p], v_recv.at[step, 2, p], dev_left),
            remote(vsend.at[step, 1, p], vrecv.at[step, 0, p], v_send.at[step, 3, p], v_recv.at[step, 3, p], dev_right),
        )

    def start_rows(step, p, src):
        up, down = v_copies(step, p, src)[:2]

        @pl.when(has_above)
        def _():
            up.start()

        @pl.when(has_below)
        def _():
            down.start()

    def start_edges(step, p, src):
        left, right = v_copies(step, p, src)[2:]
        flipped = jnp.concatenate([src[p], jnp.zeros((wide - rows_p, 128), f32)], 0).T
        vsend[step, 0, p] = flipped[:8]
        vsend[step, 1, p] = flipped[120:]
        left.start()
        right.start()

    def halo_copies(j):
        return (
            remote(kmid.at[1, part_of(j)], khalo.at[0, part_of(j)], halo_send.at[0, j], halo_recv.at[0, j], dev_above),
            remote(kmid.at[0, part_of(j)], khalo.at[1, part_of(j)], halo_send.at[1, j], halo_recv.at[1, j], dev_below),
        )

    def forward(j):
        up, down = halo_copies(j)
        for r in range(2):
            kmid[r, part_of(j), :] = kraw[j, :, r, :]

        @pl.when(gives_up(j))
        def _():
            up.start()

        @pl.when(gives_down(j))
        def _():
            down.start()

    edge_left = remote(ksend.at[0], krecv.at[1], edge_send.at[0], edge_recv.at[0], dev_left)
    edge_right = remote(ksend.at[1], krecv.at[0], edge_send.at[1], edge_recv.at[1], dev_right)

    def start_ends():
        for i in range(2 * n):
            flipped = kall[:, i // 2, i % 2, :].T
            ksend[0, i : i + 1] = flipped[:1]
            ksend[1, i : i + 1] = flipped[127:]
        edge_left.start()
        edge_right.start()

    def ends_copy(to):
        return remote(kpack.at[to], kends.at[z], ends_send.at[to], ends_recv.at[z], {"chaos": to})

    def pass_ends():
        edge_left.wait_recv()
        edge_right.wait_recv()
        for j in range(n):
            kpack[j, :2] = krecv[0, 2 * j : 2 * j + 2]
            kpack[j, 2:6] = jnp.zeros((4, pts), f32)
            kpack[j, 6:] = krecv[1, 2 * j : 2 * j + 2]
        kends[z] = kpack[z]
        for i in range(n - 1):
            ends_copy(partner(i)).start()

    get_lam.wait()
    for p in range(2):
        lam0[p, :modes] = lam_raw[:, p, :]
        lam0[p, modes:] = jnp.zeros((rows_p - modes, 128), f32)
    for p in range(2):
        start_edges(0, p, lam0)
    start_ends()
    get_own.wait()
    forward(z)

    v_cat[...] = jnp.zeros(v_cat.shape, bf16)
    e_cat[...] = jnp.zeros(e_cat.shape, bf16)

    @pl.when(jnp.logical_not(has_below))
    def _():
        khalo[0] = jnp.zeros((points, 128), f32)
        vhalo[:, 0] = jnp.zeros((STEPS, 2, rows_p, 128), f32)

    @pl.when(jnp.logical_not(has_above))
    def _():
        khalo[1] = jnp.zeros((points, 128), f32)
        vhalo[:, 1] = jnp.zeros((STEPS, 2, rows_p, 128), f32)

    def tables():
        get_quad.wait()
        get_mode.wait()
        quad = quad_ref[...]
        each = jnp.where((quad == 0) | (quad == 3), gauss_weights[0], gauss_weights[1]).astype(f32)
        wts = each[:1]
        for d in range(1, inputs):
            wts = wts * each[d : d + 1]
        wts = wts / jnp.sum(wts, axis=1, keepdims=True) * 0.25
        node = jnp.where(
            quad == 0, gauss_nodes[0],
            jnp.where(quad == 1, gauss_nodes[1], jnp.where(quad == 2, gauss_nodes[2], gauss_nodes[3])),
        ).astype(f32)
        h2 = (node * node - 1.0) * (1.0 / math.sqrt(2.0))
        h3 = (node * node * node - 3.0 * node) * (1.0 / math.sqrt(6.0))
        fill = jnp.zeros((16 - inputs, points), f32)
        one = jnp.ones((16, points), f32)
        table = jnp.concatenate([node, fill, h2, fill, h3, fill, one], 0)
        first = table.astype(bf16).astype(f32)
        rest = table - first
        second = rest.astype(bf16).astype(f32)
        third = rest - second
        pieces = jnp.concatenate([first, second, third, jnp.zeros((64, points), f32)], 0)
        by_point = pieces.T.astype(bf16)

        deg = jnp.concatenate([mode_ref[...], jnp.zeros((inputs, wide - modes), jnp.int32)], 1)
        run = jnp.zeros((1, wide), jnp.int32)
        runs = []
        for d in range(inputs):
            run = run + jnp.where(deg[d : d + 1] > 0, 1, 0)
            runs.append(run)
        nth = jnp.concatenate(runs, 0)
        blank = jnp.zeros((16 - inputs, wide), f32)
        real = lax.broadcasted_iota(jnp.int32, (1, wide), 1) < modes
        product = None
        for i in range(FACTORS):
            picks = []
            for k in range(1, 4):
                picks.append(jnp.where((deg == k) & (nth == i + 1), 1.0, 0.0).astype(f32))
                picks.append(blank)
            picks.append(jnp.where((run <= i) & real, 1.0, 0.0).astype(f32))
            picks.append(jnp.zeros((15, wide), f32))
            pick = jnp.concatenate(picks, 0)
            pick = jnp.concatenate([pick, pick, pick, jnp.zeros((64, wide), f32)], 0).astype(bf16)
            factor = jnp.dot(by_point, pick, preferred_element_type=f32)
            product = factor if product is None else product * factor
        high, low = split(product)
        psi[:, :full] = high[:, :full]
        psi[:, full : 2 * full] = low[:, :full]
        psi[:, 2 * full : 3 * full] = high[:, :full]
        if tail:
            high_end = high[:, full:].astype(f32)
            low_end = low[:, full:].astype(f32)
            psi[:, 3 * full :] = (
                high_end + pltpu.roll(low_end, tail, 1) + pltpu.roll(high_end, 2 * tail, 1)
            ).astype(bf16)
        for i in range(points // 128):
            part = slice(i * 128, i * 128 + 128)
            flipped = product[part].T[:rows_p] * wts[:, part]
            high, low = split(flipped)
            bt_h[:, part] = high
            bt_l[:, part] = low

    tables()

    lane = lax.broadcasted_iota(jnp.int32, (1, 128), 1)
    is_first, is_last = lane == 0, lane == 127
    ends = is_first | is_last

    def to_points(at, first, second):
        vh, vl = split(jnp.concatenate([first, second], 1))
        v_cat[at, :full] = vh[:full]
        v_cat[at, full : 2 * full] = vh[:full]
        v_cat[at, 2 * full : 3 * full] = vl[:full]
        if tail:
            v_cat[at, 3 * full : 3 * full + tail] = vh[full:]
            v_cat[at, 3 * full + tail : 3 * full + 2 * tail] = vh[full:]
            v_cat[at, 3 * full + 2 * tail : 3 * full + 3 * tail] = vl[full:]
        return dot(psi[...], v_cat[at])

    def step_over(v):
        return jnp.where(is_last, 0.0, pltpu.roll(v, 127, 1)) - jnp.where(is_first, 0.0, pltpu.roll(v, 1, 1))

    def own(src):
        g_in[...] = to_points(0, step_over(src[0]), step_over(src[1]))

    def wait_sides(step, p, src):
        left, right = v_copies(step, p, src)[2:]
        left.wait_recv()
        right.wait_recv()

    def wait_rows(step, p, src):
        up, down = v_copies(step, p, src)[:2]

        @pl.when(has_below)
        def _():
            up.wait_recv()

        @pl.when(has_above)
        def _():
            down.wait_recv()

    def own_ends(step, p):
        def stacked(tile):
            high, low = split(tile)
            parts = [high[:, :full], high[:, :full], low[:, :full]]
            if tail:
                high_end = high[:, full:].astype(f32)
                low_end = low[:, full:].astype(f32)
                end = high_end + pltpu.roll(high_end, tail, 1) + pltpu.roll(low_end, 2 * tail, 1)
                parts.append(end.astype(bf16))
            return jnp.concatenate(parts, 1)

        row = lax.broadcasted_iota(jnp.int32, (8, wide), 0)
        none = jnp.zeros((8, wide), f32)
        from_left, from_right = vrecv[step, 0, p], vrecv[step, 1, p]
        first, last = vsend[step, 0, p], vsend[step, 1, p]
        near = jnp.where(row == 0, -pltpu.roll(from_left, 1, 0), 0.0)
        far = jnp.where(row == 0, pltpu.roll(from_left, 2, 0) - first, 0.0)
        e_cat[p, :16] = stacked(jnp.concatenate([near, none], 0))
        e_cat[p, 128:144] = stacked(jnp.concatenate([far, none], 0))
        near = jnp.where(row == 7, pltpu.roll(from_right, 7, 0), 0.0)
        far = jnp.where(row == 7, pltpu.roll(from_right, 6, 0) - last, 0.0)
        e_cat[p, 112:128] = stacked(jnp.concatenate([none, near], 0))
        e_cat[p, 240:] = stacked(jnp.concatenate([none, far], 0))
        got = lax.dot_general(psi[...], e_cat[p], (((1,), (1,)), ((), ())), preferred_element_type=f32)
        g_x[p] = g_in[:, p * 128 : p * 128 + 128] + got[:, :128]
        g_e[p] = got[:, 128:]

    def beside(step, p, src):
        mid = src[p]
        g_y[p] = to_points(1 + p, mid - vhalo[step, 0, p], vhalo[step, 1, p] - mid)

    def each_part(body):
        def step(j, carry):
            body(j)
            return carry

        lax.fori_loop(0, n, step, 0, unroll=n <= 4)

    def update(p, src, store):
        k_low = khalo[0] if p == 0 else kmid[0]
        k_high = kmid[1] if p == 0 else khalo[1]
        flux = kmid[p] * g_x[p]
        rest = k_high * g_y[p, :, 128:] - k_low * g_y[p, :, :128] + kedge[p] * g_e[p]
        high, low = split(jnp.concatenate([rest, flux], 1))
        back = dot3(bt_h[...], bt_l[...], high, low)
        div = back[:, :128] + step_over(back[:, 128:])
        v = src[p, :modes]
        store(p, v + relax_rate * (adj_ref[:, p, :] - (mass_shift * v - div[:modes])))

    def receive(j):
        remote(coef_hbm.at[:, j], kraw.at[j], main_send.at[j], main_recv.at[j], {"chaos": j}).wait_recv()
        forward(j)

    def arrive(j):
        found = kends[j]
        for p in range(2):
            first, last = (found, pltpu.roll(found, 1, 0)) if p == 0 else (pltpu.roll(found, 7, 0), found)
            kedge[p, part_of(j), :] = jnp.concatenate([first, jnp.zeros((112, pts), f32), last], 0).T

    def source(i):
        k = outer_order[-1 - i]
        return lax.rem(z + n + sign * (k if k % 2 else -k), n)

    order = [z] + [source(i) for i in range(n - 1)]
    own(lam0)
    pass_ends()
    start_rows(0, 0, lam0)
    for p in range(2):
        wait_sides(0, p, lam0)
    for p in range(2):
        own_ends(0, p)
    for i in range(1, 2):
        receive(order[i])
    pl.when(inner)(lambda: start_rows(0, 1, lam0))
    for i in range(2, n):
        receive(order[i])
    pl.when(jnp.logical_not(inner))(lambda: start_rows(0, 1, lam0))
    for k in range(1, n):
        main_copy(lax.rem(z + k, n)).wait_send()
        ends_copy(lax.rem(z + k, n)).wait_send()
    edge_left.wait_send()
    edge_right.wait_send()

    for _, finish in straights:
        finish()

    def drain(copies, ups, downs):
        @pl.when(ups)
        def _():
            copies[0].wait_send()

        @pl.when(downs)
        def _():
            copies[1].wait_send()

        for copy in copies[2:]:
            copy.wait_send()

    for i in range(1, n):
        remote(kpack.at[order[i]], kends.at[order[i]], ends_send.at[order[i]], ends_recv.at[order[i]], {"chaos": order[i]}).wait_recv()
    for i in range(n):
        arrive(order[i])

    def halo_arrive(p):
        def body(j):
            up, down = halo_copies(j)
            if p == 0:
                @pl.when(has_below)
                def _():
                    up.wait_recv()
            else:
                @pl.when(has_above)
                def _():
                    down.wait_recv()

        each_part(body)

    def keep_lam(p, value):
        lam1[p, :modes] = value
        lam1[p, modes:] = jnp.zeros((rows_p - modes, 128), f32)

    def give(p, value):
        out_ref[:, p, :] = value

    get_adj.wait()
    for p in range(2):
        wait_rows(0, p, lam0)
        if p == 0:
            beside(0, p, lam0)
        halo_arrive(p)
        if p:
            beside(0, p, lam0)
        update(p, lam0, keep_lam)
        start_rows(1, p, lam1)
        start_edges(1, p, lam1)

    own(lam1)
    each_part(lambda j: drain(halo_copies(j), gives_up(j), gives_down(j)))
    for p in range(2):
        drain(v_copies(0, p, lam0), has_above, has_below)
    wait_sides(1, 0, lam1)
    wait_rows(1, 0, lam1)
    own_ends(1, 0)
    beside(1, 0, lam1)
    update(0, lam1, give)
    wait_sides(1, 1, lam1)
    wait_rows(1, 1, lam1)
    own_ends(1, 1)
    beside(1, 1, lam1)
    update(1, lam1, give)

    for p in range(2):
        drain(v_copies(1, p, lam1), has_above, has_below)


def local(mesh_sizes, lam_start, adj_source, coef_points, quad_index, mode_index):
    n, ngx, ncore = mesh_sizes
    modes = lam_start.shape[0]
    points, inputs = quad_index.shape
    pts = coef_points.shape[0]
    rows_p = -(-modes // 16) * 16
    wide = -(-modes // 128) * 128
    depth = -(-3 * rows_p // 128) * 128
    dims = (n, ncore, ngx, inputs, modes, rows_p, wide, points, pts)

    hbm = pl.BlockSpec(memory_space=pltpu.HBM)
    dma = pltpu.SemaphoreType.DMA
    out = pl.pallas_call(
        functools.partial(kernel, dims),
        out_shape=jax.ShapeDtypeStruct((modes, 2, 128), f32),
        in_specs=[hbm] * 5,
        out_specs=pl.BlockSpec(memory_space=pltpu.VMEM),
        scratch_shapes=[
            pltpu.VMEM((modes, 2, 128), f32),
            pltpu.VMEM((modes, 2, 128), f32),
            pltpu.VMEM((inputs, points), jnp.int32),
            pltpu.VMEM((inputs, modes), jnp.int32),
            pltpu.VMEM((n, pts, 2, 128), f32),
            pltpu.VMEM((pts, n, 2, 128), f32),
            pltpu.VMEM((4, pts, 128), f32),
            pltpu.VMEM((2, points, 128), f32),
            pltpu.VMEM((2, points, 128), f32),
            pltpu.VMEM((2, points, 128), f32),
            pltpu.VMEM((2, 2 * n, pts), f32),
            pltpu.VMEM((2, 2 * n, pts), f32),
            pltpu.VMEM((n, 8, pts), f32),
            pltpu.VMEM((n, 8, pts), f32),
            pltpu.VMEM((2, rows_p, 128), f32),
            pltpu.VMEM((2, rows_p, 128), f32),
            pltpu.VMEM((STEPS, 2, 2, rows_p, 128), f32),
            pltpu.VMEM((STEPS, 2, 2, 8, wide), f32),
            pltpu.VMEM((STEPS, 2, 2, 8, wide), f32),
            pltpu.VMEM((points, 256), f32),
            pltpu.VMEM((2, points, 128), f32),
            pltpu.VMEM((2, points, 128), f32),
            pltpu.VMEM((2, points, 256), f32),
            pltpu.VMEM((points, depth), bf16),
            pltpu.VMEM((rows_p, points), bf16),
            pltpu.VMEM((rows_p, points), bf16),
            pltpu.VMEM((3, depth, 256), bf16),
            pltpu.VMEM((2, 256, depth), bf16),
            dma((6,)), dma((n,)), dma((n,)), dma((4,)), dma((2, n)), dma((2, n)), dma((2,)), dma((2,)), dma((n,)), dma((n,)),
            dma((STEPS, 4, 2)), dma((STEPS, 4, 2)),
        ],
        compiler_params=pltpu.CompilerParams(
            collective_id=0, has_side_effects=True, vmem_limit_bytes=40 * 1024 * 1024
        ),
    )(*[pltpu.with_memory_space_constraint(v, pltpu.HBM) for v in (lam_start, adj_source, coef_points, quad_index.T, mode_index.T)])
    return out


def solution(mesh):
    sizes = (mesh.shape["chaos"], mesh.shape["gx"], mesh.shape["gy"])
    placed = (
        P(None, ("chaos", "gy"), "gx"),
        P(None, ("chaos", "gy"), "gx"),
        P("chaos", None, "gy", "gx"),
        P(),
        P(),
    )
    return jax.shard_map(
        functools.partial(local, sizes),
        mesh=mesh,
        in_specs=placed,
        out_specs=P(None, ("chaos", "gy"), "gx"),
        check_vma=False,
    )
```

```python
import functools
import math

import jax
import jax.numpy as jnp
from jax import lax
from jax.experimental import pallas as pl
from jax.experimental.pallas import tpu as pltpu
from jax.sharding import PartitionSpec as P

STEPS = 2
FACTORS = 3

gauss_nodes = (-2.3344142183389773, -0.7419637843027259, 0.7419637843027259, 2.3344142183389773)
gauss_weights = (0.04587585476806849, 0.4541241452319315, 0.4541241452319315, 0.04587585476806849)
mass_shift = 1.0
relax_rate = 0.2
f32 = jnp.float32
bf16 = jnp.bfloat16


def split(x):
    high = x.astype(bf16)
    return high, (x - high.astype(f32)).astype(bf16)


dot = functools.partial(jnp.dot, preferred_element_type=f32)


def dot3(ah, al, bh, bl):
    return dot(ah, bh) + (dot(ah, bl) + dot(al, bh))


def kernel(
    dims, lam_hbm, adj_hbm, coef_hbm, quad_hbm, mode_hbm, out_ref,
    lam_raw, adj_ref, quad_ref, mode_ref, kraw, kall, kfar, kmid, khalo, kedge, ksend, krecv, kpack, kends,
    lam0, lam1, vhalo, vsend, vrecv, g_in, g_x, g_e, g_y, psi, bt_h, bt_l, v_cat, e_cat,
    in_sem, main_send, main_recv, far_send, halo_send, halo_recv, edge_send, edge_recv, ends_send, ends_recv,
    v_send, v_recv,
):
    n, ncore, ngx, inputs, modes, rows_p, wide, points, pts = dims
    full = rows_p // 128 * 128
    tail = rows_p - full
    z, x, c = lax.axis_index("chaos"), lax.axis_index("gx"), lax.axis_index("gy")
    count = n * ncore
    me = z * ncore + c
    above = lax.rem(me + 1, count)
    below = lax.rem(me + count - 1, count)
    has_above, has_below = me < count - 1, me > 0
    dev_above = {"chaos": lax.div(above, ncore), "gy": lax.rem(above, ncore)}
    dev_below = {"chaos": lax.div(below, ncore), "gy": lax.rem(below, ncore)}
    dev_right = {"gx": lax.rem(x + 1, ngx)}
    dev_left = {"gx": lax.rem(x + ngx - 1, ngx)}
    half = n // 2
    top, bottom = c == ncore - 1, c == 0

    def gives_up(j):
        straight = (j == z + 1) | ((z + 1 == half) & (j > half))
        return has_above & jnp.logical_not(top & straight)

    def gives_down(j):
        straight = (j == z - 1) | ((z == half) & (j < half - 1))
        return has_below & jnp.logical_not(bottom & straight)

    def remote(src, dst, ss, rs, dev):
        return pltpu.make_async_remote_copy(
            src_ref=src, dst_ref=dst, send_sem=ss, recv_sem=rs, device_id=dev,
            device_id_type=pl.DeviceIdType.MESH,
        )

    def part_of(j):
        return pl.ds(pl.multiple_of(j * pts, pts), pts)

    get_own = pltpu.make_async_copy(coef_hbm.at[:, z], kraw.at[z], in_sem.at[0])
    get_all = pltpu.make_async_copy(coef_hbm, kall, in_sem.at[1])
    get_lam = pltpu.make_async_copy(lam_hbm, lam_raw, in_sem.at[2])
    get_quad = pltpu.make_async_copy(quad_hbm, quad_ref, in_sem.at[3])
    get_mode = pltpu.make_async_copy(mode_hbm, mode_ref, in_sem.at[4])
    get_adj = pltpu.make_async_copy(adj_hbm, adj_ref, in_sem.at[5])

    barrier = pltpu.get_barrier_semaphore()

    def greet(dev):
        pl.semaphore_signal(barrier, inc=1, device_id=dev, device_id_type=pl.DeviceIdType.MESH)

    def greet_line(i, carry):
        other = lax.rem(me + i, count)
        greet({"chaos": lax.div(other, ncore), "gy": lax.rem(other, ncore)})
        return carry

    lax.fori_loop(1, count, greet_line, 0, unroll=count <= 8)
    greet(dev_left)
    greet(dev_right)
    for get in (get_own, get_all, get_lam, get_quad, get_mode, get_adj):
        get.start()
    pl.semaphore_wait(barrier, count + 1)

    def main_copy(to):
        return remote(coef_hbm.at[:, to], kraw.at[z], main_send.at[to], main_recv.at[z], {"chaos": to})

    sign = 1 - 2 * lax.rem(z, 2)
    inner = (4 * z >= n) & (4 * z < 3 * n)
    outer_order = sorted(range(1, n), key=lambda k: (abs(2 * k - n), -k))
    inner_order = sorted(range(1, n), key=lambda k: (-abs(2 * k - n), k)) if n != 4 else [1, 2, 3]

    def partner(i):
        return lax.rem(z + n + sign * jnp.where(inner, inner_order[i], outer_order[i]), n)

    for i in range(n - 1):
        main_copy(partner(i)).start()

    def straight(slot, block, row, side, dev, cond):
        def copy():
            return remote(kfar.at[slot], khalo.at[side, part_of(z)], far_send.at[slot], halo_recv.at[side, z], dev)

        def start():
            @pl.when(cond)
            def _():
                kfar[slot] = kall[:, block, row, :]
                copy().start()

        def drain():
            @pl.when(cond)
            def _():
                copy().wait_send()

        return start, drain

    straights = (
        straight(0, lax.max(z - 1, 0), 1, 0, {"gy": 0}, top & (z > 0)),
        straight(1, lax.min(z + 1, n - 1), 0, 1, {"gy": ncore - 1}, bottom & (z < n - 1)),
        straight(2, half - 1, 1, 0, {"chaos": half, "gy": 0}, top & (z > half)),
        straight(3, half, 0, 1, {"chaos": half - 1, "gy": ncore - 1}, bottom & (z < half - 1)),
    )
    get_all.wait()
    for start, _ in straights[:3]:
        start()

    def v_copies(step, p, src):
        return (
            remote(src.at[p], vhalo.at[step, 0, p], v_send.at[step, 0, p], v_recv.at[step, 0, p], dev_above),
            remote(src.at[p], vhalo.at[step, 1, p], v_send.at[step, 1, p], v_recv.at[step, 1, p], dev_below),
            remote(vsend.at[step, 0, p], vrecv.at[step, 1, p], v_send.at[step, 2, p], v_recv.at[step, 2, p], dev_left),
            remote(vsend.at[step, 1, p], vrecv.at[step, 0, p], v_send.at[step, 3, p], v_recv.at[step, 3, p], dev_right),
        )

    def start_rows(step, p, src):
        up, down = v_copies(step, p, src)[:2]

        @pl.when(has_above)
        def _():
            up.start()

        @pl.when(has_below)
        def _():
            down.start()

    def start_edges(step, p, src):
        left, right = v_copies(step, p, src)[2:]
        flipped = jnp.concatenate([src[p], jnp.zeros((wide - rows_p, 128), f32)], 0).T
        vsend[step, 0, p] = flipped[:8]
        vsend[step, 1, p] = flipped[120:]
        left.start()
        right.start()

    def halo_copies(j):
        return (
            remote(kmid.at[1, part_of(j)], khalo.at[0, part_of(j)], halo_send.at[0, j], halo_recv.at[0, j], dev_above),
            remote(kmid.at[0, part_of(j)], khalo.at[1, part_of(j)], halo_send.at[1, j], halo_recv.at[1, j], dev_below),
        )

    def forward(j):
        up, down = halo_copies(j)
        for r in range(2):
            kmid[r, part_of(j), :] = kraw[j, :, r, :]

        @pl.when(gives_up(j))
        def _():
            up.start()

        @pl.when(gives_down(j))
        def _():
            down.start()

    edge_left = remote(ksend.at[0], krecv.at[1], edge_send.at[0], edge_recv.at[0], dev_left)
    edge_right = remote(ksend.at[1], krecv.at[0], edge_send.at[1], edge_recv.at[1], dev_right)

    def start_ends():
        for i in range(2 * n):
            flipped = kall[:, i // 2, i % 2, :].T
            ksend[0, i : i + 1] = flipped[:1]
            ksend[1, i : i + 1] = flipped[127:]
        edge_left.start()
        edge_right.start()

    def ends_copy(to):
        return remote(kpack.at[to], kends.at[z], ends_send.at[to], ends_recv.at[z], {"chaos": to})

    def pass_ends():
        edge_left.wait_recv()
        edge_right.wait_recv()
        for j in range(n):
            kpack[j, :2] = krecv[0, 2 * j : 2 * j + 2]
            kpack[j, 2:6] = jnp.zeros((4, pts), f32)
            kpack[j, 6:] = krecv[1, 2 * j : 2 * j + 2]
        kends[z] = kpack[z]
        for i in range(n - 1):
            ends_copy(partner(i)).start()

    get_lam.wait()
    for p in range(2):
        lam0[p, :modes] = lam_raw[:, p, :]
        lam0[p, modes:] = jnp.zeros((rows_p - modes, 128), f32)
    for p in range(2):
        start_edges(0, p, lam0)
    start_ends()
    get_own.wait()
    forward(z)

    v_cat[...] = jnp.zeros(v_cat.shape, bf16)
    e_cat[...] = jnp.zeros(e_cat.shape, bf16)

    @pl.when(jnp.logical_not(has_below))
    def _():
        khalo[0] = jnp.zeros((points, 128), f32)
        vhalo[:, 0] = jnp.zeros((STEPS, 2, rows_p, 128), f32)

    @pl.when(jnp.logical_not(has_above))
    def _():
        khalo[1] = jnp.zeros((points, 128), f32)
        vhalo[:, 1] = jnp.zeros((STEPS, 2, rows_p, 128), f32)

    def tables():
        get_quad.wait()
        get_mode.wait()
        quad = quad_ref[...]
        each = jnp.where((quad == 0) | (quad == 3), gauss_weights[0], gauss_weights[1]).astype(f32)
        wts = each[:1]
        for d in range(1, inputs):
            wts = wts * each[d : d + 1]
        wts = wts / jnp.sum(wts, axis=1, keepdims=True) * 0.25
        node = jnp.where(
            quad == 0, gauss_nodes[0],
            jnp.where(quad == 1, gauss_nodes[1], jnp.where(quad == 2, gauss_nodes[2], gauss_nodes[3])),
        ).astype(f32)
        h2 = (node * node - 1.0) * (1.0 / math.sqrt(2.0))
        h3 = (node * node * node - 3.0 * node) * (1.0 / math.sqrt(6.0))
        fill = jnp.zeros((16 - inputs, points), f32)
        one = jnp.ones((16, points), f32)
        table = jnp.concatenate([node, fill, h2, fill, h3, fill, one], 0)
        first = table.astype(bf16).astype(f32)
        rest = table - first
        second = rest.astype(bf16).astype(f32)
        third = rest - second
        pieces = jnp.concatenate([first, second, third, jnp.zeros((64, points), f32)], 0)
        by_point = pieces.T.astype(bf16)

        deg = jnp.concatenate([mode_ref[...], jnp.zeros((inputs, wide - modes), jnp.int32)], 1)
        run = jnp.zeros((1, wide), jnp.int32)
        runs = []
        for d in range(inputs):
            run = run + jnp.where(deg[d : d + 1] > 0, 1, 0)
            runs.append(run)
        nth = jnp.concatenate(runs, 0)
        blank = jnp.zeros((16 - inputs, wide), f32)
        real = lax.broadcasted_iota(jnp.int32, (1, wide), 1) < modes
        product = None
        for i in range(FACTORS):
            picks = []
            for k in range(1, 4):
                picks.append(jnp.where((deg == k) & (nth == i + 1), 1.0, 0.0).astype(f32))
                picks.append(blank)
            picks.append(jnp.where((run <= i) & real, 1.0, 0.0).astype(f32))
            picks.append(jnp.zeros((15, wide), f32))
            pick = jnp.concatenate(picks, 0)
            pick = jnp.concatenate([pick, pick, pick, jnp.zeros((64, wide), f32)], 0).astype(bf16)
            factor = jnp.dot(by_point, pick, preferred_element_type=f32)
            product = factor if product is None else product * factor
        high, low = split(product)
        psi[:, :full] = high[:, :full]
        psi[:, full : 2 * full] = low[:, :full]
        psi[:, 2 * full : 3 * full] = high[:, :full]
        if tail:
            high_end = high[:, full:].astype(f32)
            low_end = low[:, full:].astype(f32)
            psi[:, 3 * full :] = (
                high_end + pltpu.roll(low_end, tail, 1) + pltpu.roll(high_end, 2 * tail, 1)
            ).astype(bf16)
        for i in range(points // 128):
            part = slice(i * 128, i * 128 + 128)
            flipped = product[part].T[:rows_p] * wts[:, part]
            high, low = split(flipped)
            bt_h[:, part] = high
            bt_l[:, part] = low

    tables()

    lane = lax.broadcasted_iota(jnp.int32, (1, 128), 1)
    is_first, is_last = lane == 0, lane == 127
    ends = is_first | is_last

    def to_points(at, first, second):
        vh, vl = split(jnp.concatenate([first, second], 1))
        v_cat[at, :full] = vh[:full]
        v_cat[at, full : 2 * full] = vh[:full]
        v_cat[at, 2 * full : 3 * full] = vl[:full]
        if tail:
            v_cat[at, 3 * full : 3 * full + tail] = vh[full:]
            v_cat[at, 3 * full + tail : 3 * full + 2 * tail] = vh[full:]
            v_cat[at, 3 * full + 2 * tail : 3 * full + 3 * tail] = vl[full:]
        return dot(psi[...], v_cat[at])

    def step_over(v):
        return jnp.where(is_last, 0.0, pltpu.roll(v, 127, 1)) - jnp.where(is_first, 0.0, pltpu.roll(v, 1, 1))

    def own(src):
        g_in[...] = to_points(0, step_over(src[0]), step_over(src[1]))

    def wait_sides(step, p, src):
        left, right = v_copies(step, p, src)[2:]
        left.wait_recv()
        right.wait_recv()

    def wait_rows(step, p, src):
        up, down = v_copies(step, p, src)[:2]

        @pl.when(has_below)
        def _():
            up.wait_recv()

        @pl.when(has_above)
        def _():
            down.wait_recv()

    def own_ends(step, p):
        def stacked(tile):
            high, low = split(tile)
            parts = [high[:, :full], high[:, :full], low[:, :full]]
            if tail:
                high_end = high[:, full:].astype(f32)
                low_end = low[:, full:].astype(f32)
                end = high_end + pltpu.roll(high_end, tail, 1) + pltpu.roll(low_end, 2 * tail, 1)
                parts.append(end.astype(bf16))
            return jnp.concatenate(parts, 1)

        row = lax.broadcasted_iota(jnp.int32, (8, wide), 0)
        none = jnp.zeros((8, wide), f32)
        from_left, from_right = vrecv[step, 0, p], vrecv[step, 1, p]
        first, last = vsend[step, 0, p], vsend[step, 1, p]
        near = jnp.where(row == 0, -pltpu.roll(from_left, 1, 0), 0.0)
        far = jnp.where(row == 0, pltpu.roll(from_left, 2, 0) - first, 0.0)
        e_cat[p, :16] = stacked(jnp.concatenate([near, none], 0))
        e_cat[p, 128:144] = stacked(jnp.concatenate([far, none], 0))
        near = jnp.where(row == 7, pltpu.roll(from_right, 7, 0), 0.0)
        far = jnp.where(row == 7, pltpu.roll(from_right, 6, 0) - last, 0.0)
        e_cat[p, 112:128] = stacked(jnp.concatenate([none, near], 0))
        e_cat[p, 240:] = stacked(jnp.concatenate([none, far], 0))
        got = lax.dot_general(psi[...], e_cat[p], (((1,), (1,)), ((), ())), preferred_element_type=f32)
        g_x[p] = g_in[:, p * 128 : p * 128 + 128] + got[:, :128]
        g_e[p] = got[:, 128:]

    def beside(step, p, src):
        mid = src[p]
        g_y[p] = to_points(1 + p, mid - vhalo[step, 0, p], vhalo[step, 1, p] - mid)

    def each_part(body):
        def step(j, carry):
            body(j)
            return carry

        lax.fori_loop(0, n, step, 0, unroll=n <= 4)

    def update(p, src, store):
        k_low = khalo[0] if p == 0 else kmid[0]
        k_high = kmid[1] if p == 0 else khalo[1]
        flux = kmid[p] * g_x[p]
        rest = k_high * g_y[p, :, 128:] - k_low * g_y[p, :, :128] + kedge[p] * g_e[p]
        high, low = split(jnp.concatenate([rest, flux], 1))
        back = dot3(bt_h[...], bt_l[...], high, low)
        div = back[:, :128] + step_over(back[:, 128:])
        v = src[p, :modes]
        store(p, v + relax_rate * (adj_ref[:, p, :] - (mass_shift * v - div[:modes])))

    def receive(j):
        remote(coef_hbm.at[:, j], kraw.at[j], main_send.at[j], main_recv.at[j], {"chaos": j}).wait_recv()
        forward(j)

    def arrive(j):
        found = kends[j]
        for p in range(2):
            first, last = (found, pltpu.roll(found, 1, 0)) if p == 0 else (pltpu.roll(found, 7, 0), found)
            kedge[p, part_of(j), :] = jnp.concatenate([first, jnp.zeros((112, pts), f32), last], 0).T

    def source(i):
        k = outer_order[-1 - i]
        return lax.rem(z + n + sign * (k if k % 2 else -k), n)

    order = [z] + [source(i) for i in range(n - 1)]
    own(lam0)
    pass_ends()
    start_rows(0, 0, lam0)
    for p in range(2):
        wait_sides(0, p, lam0)
    for p in range(2):
        own_ends(0, p)
    for i in range(1, 2):
        receive(order[i])
    straights[3][0]()
    pl.when(inner)(lambda: start_rows(0, 1, lam0))
    for i in range(2, n):
        receive(order[i])
    pl.when(jnp.logical_not(inner))(lambda: start_rows(0, 1, lam0))
    for k in range(1, n):
        main_copy(lax.rem(z + k, n)).wait_send()
        ends_copy(lax.rem(z + k, n)).wait_send()
    edge_left.wait_send()
    edge_right.wait_send()

    for _, finish in straights:
        finish()

    def drain(copies, ups, downs):
        @pl.when(ups)
        def _():
            copies[0].wait_send()

        @pl.when(downs)
        def _():
            copies[1].wait_send()

        for copy in copies[2:]:
            copy.wait_send()

    for i in range(1, n):
        remote(kpack.at[order[i]], kends.at[order[i]], ends_send.at[order[i]], ends_recv.at[order[i]], {"chaos": order[i]}).wait_recv()
    for i in range(n):
        arrive(order[i])

    def halo_arrive(p):
        def body(j):
            up, down = halo_copies(j)
            if p == 0:
                @pl.when(has_below)
                def _():
                    up.wait_recv()
            else:
                @pl.when(has_above)
                def _():
                    down.wait_recv()

        each_part(body)

    def keep_lam(p, value):
        lam1[p, :modes] = value
        lam1[p, modes:] = jnp.zeros((rows_p - modes, 128), f32)

    def give(p, value):
        out_ref[:, p, :] = value

    get_adj.wait()
    for p in range(2):
        wait_rows(0, p, lam0)
        if p == 0:
            beside(0, p, lam0)
        halo_arrive(p)
        if p:
            beside(0, p, lam0)
        update(p, lam0, keep_lam)
        start_rows(1, p, lam1)
        start_edges(1, p, lam1)

    own(lam1)
    each_part(lambda j: drain(halo_copies(j), gives_up(j), gives_down(j)))
    for p in range(2):
        drain(v_copies(0, p, lam0), has_above, has_below)
    wait_sides(1, 0, lam1)
    wait_rows(1, 0, lam1)
    own_ends(1, 0)
    beside(1, 0, lam1)
    update(0, lam1, give)
    wait_sides(1, 1, lam1)
    wait_rows(1, 1, lam1)
    own_ends(1, 1)
    beside(1, 1, lam1)
    update(1, lam1, give)

    for p in range(2):
        drain(v_copies(1, p, lam1), has_above, has_below)


def local(mesh_sizes, lam_start, adj_source, coef_points, quad_index, mode_index):
    n, ngx, ncore = mesh_sizes
    modes = lam_start.shape[0]
    points, inputs = quad_index.shape
    pts = coef_points.shape[0]
    rows_p = -(-modes // 16) * 16
    wide = -(-modes // 128) * 128
    depth = -(-3 * rows_p // 128) * 128
    dims = (n, ncore, ngx, inputs, modes, rows_p, wide, points, pts)

    hbm = pl.BlockSpec(memory_space=pltpu.HBM)
    dma = pltpu.SemaphoreType.DMA
    out = pl.pallas_call(
        functools.partial(kernel, dims),
        out_shape=jax.ShapeDtypeStruct((modes, 2, 128), f32),
        in_specs=[hbm] * 5,
        out_specs=pl.BlockSpec(memory_space=pltpu.VMEM),
        scratch_shapes=[
            pltpu.VMEM((modes, 2, 128), f32),
            pltpu.VMEM((modes, 2, 128), f32),
            pltpu.VMEM((inputs, points), jnp.int32),
            pltpu.VMEM((inputs, modes), jnp.int32),
            pltpu.VMEM((n, pts, 2, 128), f32),
            pltpu.VMEM((pts, n, 2, 128), f32),
            pltpu.VMEM((4, pts, 128), f32),
            pltpu.VMEM((2, points, 128), f32),
            pltpu.VMEM((2, points, 128), f32),
            pltpu.VMEM((2, points, 128), f32),
            pltpu.VMEM((2, 2 * n, pts), f32),
            pltpu.VMEM((2, 2 * n, pts), f32),
            pltpu.VMEM((n, 8, pts), f32),
            pltpu.VMEM((n, 8, pts), f32),
            pltpu.VMEM((2, rows_p, 128), f32),
            pltpu.VMEM((2, rows_p, 128), f32),
            pltpu.VMEM((STEPS, 2, 2, rows_p, 128), f32),
            pltpu.VMEM((STEPS, 2, 2, 8, wide), f32),
            pltpu.VMEM((STEPS, 2, 2, 8, wide), f32),
            pltpu.VMEM((points, 256), f32),
            pltpu.VMEM((2, points, 128), f32),
            pltpu.VMEM((2, points, 128), f32),
            pltpu.VMEM((2, points, 256), f32),
            pltpu.VMEM((points, depth), bf16),
            pltpu.VMEM((rows_p, points), bf16),
            pltpu.VMEM((rows_p, points), bf16),
            pltpu.VMEM((3, depth, 256), bf16),
            pltpu.VMEM((2, 256, depth), bf16),
            dma((6,)), dma((n,)), dma((n,)), dma((4,)), dma((2, n)), dma((2, n)), dma((2,)), dma((2,)), dma((n,)), dma((n,)),
            dma((STEPS, 4, 2)), dma((STEPS, 4, 2)),
        ],
        compiler_params=pltpu.CompilerParams(
            collective_id=0, has_side_effects=True, vmem_limit_bytes=40 * 1024 * 1024
        ),
    )(*[pltpu.with_memory_space_constraint(v, pltpu.HBM) for v in (lam_start, adj_source, coef_points, quad_index.T, mode_index.T)])
    return out


def solution(mesh):
    sizes = (mesh.shape["chaos"], mesh.shape["gx"], mesh.shape["gy"])
    placed = (
        P(None, ("chaos", "gy"), "gx"),
        P(None, ("chaos", "gy"), "gx"),
        P("chaos", None, "gy", "gx"),
        P(),
        P(),
    )
    return jax.shard_map(
        functools.partial(local, sizes),
        mesh=mesh,
        in_specs=placed,
        out_specs=P(None, ("chaos", "gy"), "gx"),
        check_vma=False,
    )
```

```python
import functools
import math

import jax
import jax.numpy as jnp
from jax import lax
from jax.experimental import pallas as pl
from jax.experimental.pallas import tpu as pltpu
from jax.sharding import PartitionSpec as P

STEPS = 2
FACTORS = 3

gauss_nodes = (-2.3344142183389773, -0.7419637843027259, 0.7419637843027259, 2.3344142183389773)
gauss_weights = (0.04587585476806849, 0.4541241452319315, 0.4541241452319315, 0.04587585476806849)
mass_shift = 1.0
relax_rate = 0.2
f32 = jnp.float32
bf16 = jnp.bfloat16


def split(x):
    high = x.astype(bf16)
    return high, (x - high.astype(f32)).astype(bf16)


dot = functools.partial(jnp.dot, preferred_element_type=f32)


def dot3(ah, al, bh, bl):
    return dot(ah, bh) + (dot(ah, bl) + dot(al, bh))


def kernel(
    dims, lam_hbm, adj_hbm, coef_hbm, quad_hbm, mode_hbm, out_ref,
    lam_raw, adj_ref, quad_ref, mode_ref, kraw, kall, kfar, kmid, khalo, kedge, ksend, krecv, kpack, kends,
    lam0, lam1, vhalo, vsend, vrecv, g_in, g_x, g_e, g_y, psi, bt_h, bt_l, v_cat, e_cat,
    in_sem, main_send, main_recv, far_send, halo_send, halo_recv, edge_send, edge_recv, ends_send, ends_recv,
    v_send, v_recv,
):
    n, ncore, ngx, inputs, modes, rows_p, wide, points, pts = dims
    full = rows_p // 128 * 128
    tail = rows_p - full
    z, x, c = lax.axis_index("chaos"), lax.axis_index("gx"), lax.axis_index("gy")
    count = n * ncore
    me = z * ncore + c
    above = lax.rem(me + 1, count)
    below = lax.rem(me + count - 1, count)
    has_above, has_below = me < count - 1, me > 0
    dev_above = {"chaos": lax.div(above, ncore), "gy": lax.rem(above, ncore)}
    dev_below = {"chaos": lax.div(below, ncore), "gy": lax.rem(below, ncore)}
    dev_right = {"gx": lax.rem(x + 1, ngx)}
    dev_left = {"gx": lax.rem(x + ngx - 1, ngx)}
    half = n // 2
    top, bottom = c == ncore - 1, c == 0

    def gives_up(j):
        straight = (j == z + 1) | ((z + 1 == half) & (j > half))
        return has_above & jnp.logical_not(top & straight)

    def gives_down(j):
        straight = (j == z - 1) | ((z == half) & (j < half - 1))
        return has_below & jnp.logical_not(bottom & straight)

    def remote(src, dst, ss, rs, dev):
        return pltpu.make_async_remote_copy(
            src_ref=src, dst_ref=dst, send_sem=ss, recv_sem=rs, device_id=dev,
            device_id_type=pl.DeviceIdType.MESH,
        )

    def part_of(j):
        return pl.ds(pl.multiple_of(j * pts, pts), pts)

    get_own = pltpu.make_async_copy(coef_hbm.at[:, z], kraw.at[z], in_sem.at[0])
    get_all = pltpu.make_async_copy(coef_hbm, kall, in_sem.at[1])
    get_lam = pltpu.make_async_copy(lam_hbm, lam_raw, in_sem.at[2])
    get_quad = pltpu.make_async_copy(quad_hbm, quad_ref, in_sem.at[3])
    get_mode = pltpu.make_async_copy(mode_hbm, mode_ref, in_sem.at[4])
    get_adj = pltpu.make_async_copy(adj_hbm, adj_ref, in_sem.at[5])

    barrier = pltpu.get_barrier_semaphore()

    def greet(dev):
        pl.semaphore_signal(barrier, inc=1, device_id=dev, device_id_type=pl.DeviceIdType.MESH)

    def greet_line(i, carry):
        other = lax.rem(me + i, count)
        greet({"chaos": lax.div(other, ncore), "gy": lax.rem(other, ncore)})
        return carry

    lax.fori_loop(1, count, greet_line, 0, unroll=count <= 8)
    greet(dev_left)
    greet(dev_right)
    for get in (get_own, get_all, get_lam, get_quad, get_mode, get_adj):
        get.start()
    pl.semaphore_wait(barrier, count + 1)

    def main_copy(to):
        return remote(coef_hbm.at[:, to], kraw.at[z], main_send.at[to], main_recv.at[z], {"chaos": to})

    sign = 1 - 2 * lax.rem(z, 2)
    inner = (4 * z >= n) & (4 * z < 3 * n)
    outer_order = sorted(range(1, n), key=lambda k: (abs(2 * k - n), -k))
    inner_order = sorted(range(1, n), key=lambda k: (-abs(2 * k - n), k)) if n != 4 else [1, 2, 3]

    def partner(i):
        return lax.rem(z + n + sign * jnp.where(inner, inner_order[i], outer_order[i]), n)

    for i in range(n - 1):
        main_copy(partner(i)).start()

    def straight(slot, block, row, side, dev, cond):
        def copy():
            return remote(kfar.at[slot], khalo.at[side, part_of(z)], far_send.at[slot], halo_recv.at[side, z], dev)

        def start():
            @pl.when(cond)
            def _():
                kfar[slot] = kall[:, block, row, :]
                copy().start()

        def drain():
            @pl.when(cond)
            def _():
                copy().wait_send()

        return start, drain

    straights = (
        straight(0, lax.max(z - 1, 0), 1, 0, {"gy": 0}, top & (z > 0)),
        straight(1, lax.min(z + 1, n - 1), 0, 1, {"gy": ncore - 1}, bottom & (z < n - 1)),
        straight(2, half - 1, 1, 0, {"chaos": half, "gy": 0}, top & (z > half)),
        straight(3, half, 0, 1, {"chaos": half - 1, "gy": ncore - 1}, bottom & (z < half - 1)),
    )
    get_all.wait()
    for start, _ in straights[:3]:
        start()

    def v_copies(step, p, src):
        return (
            remote(src.at[p], vhalo.at[step, 0, p], v_send.at[step, 0, p], v_recv.at[step, 0, p], dev_above),
            remote(src.at[p], vhalo.at[step, 1, p], v_send.at[step, 1, p], v_recv.at[step, 1, p], dev_below),
            remote(vsend.at[step, 0, p], vrecv.at[step, 1, p], v_send.at[step, 2, p], v_recv.at[step, 2, p], dev_left),
            remote(vsend.at[step, 1, p], vrecv.at[step, 0, p], v_send.at[step, 3, p], v_recv.at[step, 3, p], dev_right),
        )

    def start_rows(step, p, src):
        up, down = v_copies(step, p, src)[:2]

        @pl.when(has_above)
        def _():
            up.start()

        @pl.when(has_below)
        def _():
            down.start()

    def start_edges(step, p, src):
        left, right = v_copies(step, p, src)[2:]
        flipped = jnp.concatenate([src[p], jnp.zeros((wide - rows_p, 128), f32)], 0).T
        vsend[step, 0, p] = flipped[:8]
        vsend[step, 1, p] = flipped[120:]
        left.start()
        right.start()

    def halo_copies(j):
        return (
            remote(kmid.at[1, part_of(j)], khalo.at[0, part_of(j)], halo_send.at[0, j], halo_recv.at[0, j], dev_above),
            remote(kmid.at[0, part_of(j)], khalo.at[1, part_of(j)], halo_send.at[1, j], halo_recv.at[1, j], dev_below),
        )

    def forward(j):
        up, down = halo_copies(j)
        for r in range(2):
            kmid[r, part_of(j), :] = kraw[j, :, r, :]

        @pl.when(gives_up(j))
        def _():
            up.start()

        @pl.when(gives_down(j))
        def _():
            down.start()

    edge_left = remote(ksend.at[0], krecv.at[1], edge_send.at[0], edge_recv.at[0], dev_left)
    edge_right = remote(ksend.at[1], krecv.at[0], edge_send.at[1], edge_recv.at[1], dev_right)

    def start_ends():
        for i in range(2 * n):
            flipped = kall[:, i // 2, i % 2, :].T
            ksend[0, i : i + 1] = flipped[:1]
            ksend[1, i : i + 1] = flipped[127:]
        edge_left.start()
        edge_right.start()

    def ends_copy(to):
        return remote(kpack.at[to], kends.at[z], ends_send.at[to], ends_recv.at[z], {"chaos": to})

    def pass_ends():
        edge_left.wait_recv()
        edge_right.wait_recv()
        for j in range(n):
            kpack[j, :2] = krecv[0, 2 * j : 2 * j + 2]
            kpack[j, 2:6] = jnp.zeros((4, pts), f32)
            kpack[j, 6:] = krecv[1, 2 * j : 2 * j + 2]
        kends[z] = kpack[z]
        for i in range(n - 1):
            ends_copy(partner(i)).start()

    get_lam.wait()
    for p in range(2):
        lam0[p, :modes] = lam_raw[:, p, :]
        lam0[p, modes:] = jnp.zeros((rows_p - modes, 128), f32)
    for p in range(2):
        start_edges(0, p, lam0)
    start_ends()
    get_own.wait()
    forward(z)

    v_cat[...] = jnp.zeros(v_cat.shape, bf16)
    e_cat[...] = jnp.zeros(e_cat.shape, bf16)

    @pl.when(jnp.logical_not(has_below))
    def _():
        khalo[0] = jnp.zeros((points, 128), f32)
        vhalo[:, 0] = jnp.zeros((STEPS, 2, rows_p, 128), f32)

    @pl.when(jnp.logical_not(has_above))
    def _():
        khalo[1] = jnp.zeros((points, 128), f32)
        vhalo[:, 1] = jnp.zeros((STEPS, 2, rows_p, 128), f32)

    def tables():
        get_quad.wait()
        get_mode.wait()
        quad = quad_ref[...]
        each = jnp.where((quad == 0) | (quad == 3), gauss_weights[0], gauss_weights[1]).astype(f32)
        wts = each[:1]
        for d in range(1, inputs):
            wts = wts * each[d : d + 1]
        wts = wts / jnp.sum(wts, axis=1, keepdims=True) * 0.25
        node = jnp.where(
            quad == 0, gauss_nodes[0],
            jnp.where(quad == 1, gauss_nodes[1], jnp.where(quad == 2, gauss_nodes[2], gauss_nodes[3])),
        ).astype(f32)
        h2 = (node * node - 1.0) * (1.0 / math.sqrt(2.0))
        h3 = (node * node * node - 3.0 * node) * (1.0 / math.sqrt(6.0))
        fill = jnp.zeros((16 - inputs, points), f32)
        one = jnp.ones((16, points), f32)
        table = jnp.concatenate([node, fill, h2, fill, h3, fill, one], 0)
        first = table.astype(bf16).astype(f32)
        rest = table - first
        second = rest.astype(bf16).astype(f32)
        third = rest - second
        pieces = jnp.concatenate([first, second, third, jnp.zeros((64, points), f32)], 0)
        by_point = pieces.T.astype(bf16)

        deg = jnp.concatenate([mode_ref[...], jnp.zeros((inputs, wide - modes), jnp.int32)], 1)
        run = jnp.zeros((1, wide), jnp.int32)
        runs = []
        for d in range(inputs):
            run = run + jnp.where(deg[d : d + 1] > 0, 1, 0)
            runs.append(run)
        nth = jnp.concatenate(runs, 0)
        blank = jnp.zeros((16 - inputs, wide), f32)
        real = lax.broadcasted_iota(jnp.int32, (1, wide), 1) < modes
        product = None
        for i in range(FACTORS):
            picks = []
            for k in range(1, 4):
                picks.append(jnp.where((deg == k) & (nth == i + 1), 1.0, 0.0).astype(f32))
                picks.append(blank)
            picks.append(jnp.where((run <= i) & real, 1.0, 0.0).astype(f32))
            picks.append(jnp.zeros((15, wide), f32))
            pick = jnp.concatenate(picks, 0)
            pick = jnp.concatenate([pick, pick, pick, jnp.zeros((64, wide), f32)], 0).astype(bf16)
            factor = jnp.dot(by_point, pick, preferred_element_type=f32)
            product = factor if product is None else product * factor
        high, low = split(product)
        psi[:, :full] = high[:, :full]
        psi[:, full : 2 * full] = low[:, :full]
        psi[:, 2 * full : 3 * full] = high[:, :full]
        if tail:
            high_end = high[:, full:].astype(f32)
            low_end = low[:, full:].astype(f32)
            psi[:, 3 * full :] = (
                high_end + pltpu.roll(low_end, tail, 1) + pltpu.roll(high_end, 2 * tail, 1)
            ).astype(bf16)
        for i in range(points // 128):
            part = slice(i * 128, i * 128 + 128)
            flipped = product[part].T[:rows_p] * wts[:, part]
            high, low = split(flipped)
            bt_h[:, part] = high
            bt_l[:, part] = low

    tables()

    lane = lax.broadcasted_iota(jnp.int32, (1, 128), 1)
    is_first, is_last = lane == 0, lane == 127
    ends = is_first | is_last

    def to_points(at, first, second):
        vh, vl = split(jnp.concatenate([first, second], 1))
        v_cat[at, :full] = vh[:full]
        v_cat[at, full : 2 * full] = vh[:full]
        v_cat[at, 2 * full : 3 * full] = vl[:full]
        if tail:
            v_cat[at, 3 * full : 3 * full + tail] = vh[full:]
            v_cat[at, 3 * full + tail : 3 * full + 2 * tail] = vh[full:]
            v_cat[at, 3 * full + 2 * tail : 3 * full + 3 * tail] = vl[full:]
        return dot(psi[...], v_cat[at])

    def step_over(v):
        return jnp.where(is_last, 0.0, pltpu.roll(v, 127, 1)) - jnp.where(is_first, 0.0, pltpu.roll(v, 1, 1))

    def own(src):
        g_in[...] = to_points(0, step_over(src[0]), step_over(src[1]))

    def wait_sides(step, p, src):
        left, right = v_copies(step, p, src)[2:]
        left.wait_recv()
        right.wait_recv()

    def wait_rows(step, p, src):
        up, down = v_copies(step, p, src)[:2]

        @pl.when(has_below)
        def _():
            up.wait_recv()

        @pl.when(has_above)
        def _():
            down.wait_recv()

    def own_ends(step, p):
        def stacked(tile):
            high, low = split(tile)
            parts = [high[:, :full], high[:, :full], low[:, :full]]
            if tail:
                high_end = high[:, full:].astype(f32)
                low_end = low[:, full:].astype(f32)
                end = high_end + pltpu.roll(high_end, tail, 1) + pltpu.roll(low_end, 2 * tail, 1)
                parts.append(end.astype(bf16))
            return jnp.concatenate(parts, 1)

        row = lax.broadcasted_iota(jnp.int32, (8, wide), 0)
        none = jnp.zeros((8, wide), f32)
        from_left, from_right = vrecv[step, 0, p], vrecv[step, 1, p]
        first, last = vsend[step, 0, p], vsend[step, 1, p]
        near = jnp.where(row == 0, -pltpu.roll(from_left, 1, 0), 0.0)
        far = jnp.where(row == 0, pltpu.roll(from_left, 2, 0) - first, 0.0)
        e_cat[p, :16] = stacked(jnp.concatenate([near, none], 0))
        e_cat[p, 128:144] = stacked(jnp.concatenate([far, none], 0))
        near = jnp.where(row == 7, pltpu.roll(from_right, 7, 0), 0.0)
        far = jnp.where(row == 7, pltpu.roll(from_right, 6, 0) - last, 0.0)
        e_cat[p, 112:128] = stacked(jnp.concatenate([none, near], 0))
        e_cat[p, 240:] = stacked(jnp.concatenate([none, far], 0))
        got = lax.dot_general(psi[...], e_cat[p], (((1,), (1,)), ((), ())), preferred_element_type=f32)
        g_x[p] = g_in[:, p * 128 : p * 128 + 128] + got[:, :128]
        g_e[p] = got[:, 128:]

    def beside(step, p, src):
        mid = src[p]
        g_y[p] = to_points(1 + p, mid - vhalo[step, 0, p], vhalo[step, 1, p] - mid)

    def each_part(body):
        def step(j, carry):
            body(j)
            return carry

        lax.fori_loop(0, n, step, 0, unroll=n <= 4)

    def update(p, src, store):
        k_low = khalo[0] if p == 0 else kmid[0]
        k_high = kmid[1] if p == 0 else khalo[1]
        flux = kmid[p] * g_x[p]
        rest = k_high * g_y[p, :, 128:] - k_low * g_y[p, :, :128] + kedge[p] * g_e[p]
        high, low = split(jnp.concatenate([rest, flux], 1))
        back = dot3(bt_h[...], bt_l[...], high, low)
        div = back[:, :128] + step_over(back[:, 128:])
        v = src[p, :modes]
        store(p, v + relax_rate * (adj_ref[:, p, :] - (mass_shift * v - div[:modes])))

    def receive(j):
        remote(coef_hbm.at[:, j], kraw.at[j], main_send.at[j], main_recv.at[j], {"chaos": j}).wait_recv()
        forward(j)

    def arrive(j):
        found = kends[j]
        for p in range(2):
            first, last = (found, pltpu.roll(found, 1, 0)) if p == 0 else (pltpu.roll(found, 7, 0), found)
            kedge[p, part_of(j), :] = jnp.concatenate([first, jnp.zeros((112, pts), f32), last], 0).T

    def source(i):
        k = outer_order[-1 - i]
        return lax.rem(z + n + sign * (k if k % 2 else -k), n)

    order = [z] + [source(i) for i in range(n - 1)]
    own(lam0)
    pass_ends()
    pl.when(inner)(lambda: start_rows(0, 0, lam0))
    for p in range(2):
        wait_sides(0, p, lam0)
    for p in range(2):
        own_ends(0, p)
    for i in range(1, 2):
        receive(order[i])
    straights[3][0]()
    pl.when(inner)(lambda: start_rows(0, 1, lam0))
    pl.when(jnp.logical_not(inner))(lambda: start_rows(0, 0, lam0))
    for i in range(2, n):
        receive(order[i])
    pl.when(jnp.logical_not(inner))(lambda: start_rows(0, 1, lam0))
    for k in range(1, n):
        main_copy(lax.rem(z + k, n)).wait_send()
        ends_copy(lax.rem(z + k, n)).wait_send()
    edge_left.wait_send()
    edge_right.wait_send()

    for _, finish in straights:
        finish()

    def drain(copies, ups, downs):
        @pl.when(ups)
        def _():
            copies[0].wait_send()

        @pl.when(downs)
        def _():
            copies[1].wait_send()

        for copy in copies[2:]:
            copy.wait_send()

    for i in range(1, n):
        remote(kpack.at[order[i]], kends.at[order[i]], ends_send.at[order[i]], ends_recv.at[order[i]], {"chaos": order[i]}).wait_recv()
    for i in range(n):
        arrive(order[i])

    def halo_arrive(p):
        def body(j):
            up, down = halo_copies(j)
            if p == 0:
                @pl.when(has_below)
                def _():
                    up.wait_recv()
            else:
                @pl.when(has_above)
                def _():
                    down.wait_recv()

        each_part(body)

    def keep_lam(p, value):
        lam1[p, :modes] = value
        lam1[p, modes:] = jnp.zeros((rows_p - modes, 128), f32)

    def give(p, value):
        out_ref[:, p, :] = value

    get_adj.wait()
    for p in range(2):
        wait_rows(0, p, lam0)
        if p == 0:
            beside(0, p, lam0)
        halo_arrive(p)
        if p:
            beside(0, p, lam0)
        update(p, lam0, keep_lam)
        start_rows(1, p, lam1)
        start_edges(1, p, lam1)

    own(lam1)
    each_part(lambda j: drain(halo_copies(j), gives_up(j), gives_down(j)))
    for p in range(2):
        drain(v_copies(0, p, lam0), has_above, has_below)
    wait_sides(1, 0, lam1)
    wait_rows(1, 0, lam1)
    own_ends(1, 0)
    beside(1, 0, lam1)
    update(0, lam1, give)
    wait_sides(1, 1, lam1)
    wait_rows(1, 1, lam1)
    own_ends(1, 1)
    beside(1, 1, lam1)
    update(1, lam1, give)

    for p in range(2):
        drain(v_copies(1, p, lam1), has_above, has_below)


def local(mesh_sizes, lam_start, adj_source, coef_points, quad_index, mode_index):
    n, ngx, ncore = mesh_sizes
    modes = lam_start.shape[0]
    points, inputs = quad_index.shape
    pts = coef_points.shape[0]
    rows_p = -(-modes // 16) * 16
    wide = -(-modes // 128) * 128
    depth = -(-3 * rows_p // 128) * 128
    dims = (n, ncore, ngx, inputs, modes, rows_p, wide, points, pts)

    hbm = pl.BlockSpec(memory_space=pltpu.HBM)
    dma = pltpu.SemaphoreType.DMA
    out = pl.pallas_call(
        functools.partial(kernel, dims),
        out_shape=jax.ShapeDtypeStruct((modes, 2, 128), f32),
        in_specs=[hbm] * 5,
        out_specs=pl.BlockSpec(memory_space=pltpu.VMEM),
        scratch_shapes=[
            pltpu.VMEM((modes, 2, 128), f32),
            pltpu.VMEM((modes, 2, 128), f32),
            pltpu.VMEM((inputs, points), jnp.int32),
            pltpu.VMEM((inputs, modes), jnp.int32),
            pltpu.VMEM((n, pts, 2, 128), f32),
            pltpu.VMEM((pts, n, 2, 128), f32),
            pltpu.VMEM((4, pts, 128), f32),
            pltpu.VMEM((2, points, 128), f32),
            pltpu.VMEM((2, points, 128), f32),
            pltpu.VMEM((2, points, 128), f32),
            pltpu.VMEM((2, 2 * n, pts), f32),
            pltpu.VMEM((2, 2 * n, pts), f32),
            pltpu.VMEM((n, 8, pts), f32),
            pltpu.VMEM((n, 8, pts), f32),
            pltpu.VMEM((2, rows_p, 128), f32),
            pltpu.VMEM((2, rows_p, 128), f32),
            pltpu.VMEM((STEPS, 2, 2, rows_p, 128), f32),
            pltpu.VMEM((STEPS, 2, 2, 8, wide), f32),
            pltpu.VMEM((STEPS, 2, 2, 8, wide), f32),
            pltpu.VMEM((points, 256), f32),
            pltpu.VMEM((2, points, 128), f32),
            pltpu.VMEM((2, points, 128), f32),
            pltpu.VMEM((2, points, 256), f32),
            pltpu.VMEM((points, depth), bf16),
            pltpu.VMEM((rows_p, points), bf16),
            pltpu.VMEM((rows_p, points), bf16),
            pltpu.VMEM((3, depth, 256), bf16),
            pltpu.VMEM((2, 256, depth), bf16),
            dma((6,)), dma((n,)), dma((n,)), dma((4,)), dma((2, n)), dma((2, n)), dma((2,)), dma((2,)), dma((n,)), dma((n,)),
            dma((STEPS, 4, 2)), dma((STEPS, 4, 2)),
        ],
        compiler_params=pltpu.CompilerParams(
            collective_id=0, has_side_effects=True, vmem_limit_bytes=40 * 1024 * 1024
        ),
    )(*[pltpu.with_memory_space_constraint(v, pltpu.HBM) for v in (lam_start, adj_source, coef_points, quad_index.T, mode_index.T)])
    return out


def solution(mesh):
    sizes = (mesh.shape["chaos"], mesh.shape["gx"], mesh.shape["gy"])
    placed = (
        P(None, ("chaos", "gy"), "gx"),
        P(None, ("chaos", "gy"), "gx"),
        P("chaos", None, "gy", "gx"),
        P(),
        P(),
    )
    return jax.shard_map(
        functools.partial(local, sizes),
        mesh=mesh,
        in_specs=placed,
        out_specs=P(None, ("chaos", "gy"), "gx"),
        check_vma=False,
    )
```
